1024 devices in a mesh: space: 512 (over x_hi, z, y, core), dp: 2 (over x_lo).
Axes of the slice: x: 4 (x_hi: 2, x_lo: 2; x = x_hi * 2 + x_lo), y: 4, z: 32, core: 2. Of those that a mesh axis runs over, the one named last changes fastest.
Arguments:
- node_features: float32 [2, 128, 131072], P('dp', None, 'space'), may hold values from -6 to 6
- positions: float32 [2, 3, 131072], P('dp', None, 'space')
- species: int32 [2, 131072], P('dp', 'space'), may hold values from 0 to 7
- energy_cotangent: float32 [2, 131072], P('dp', 'space'), may hold values from -6 to 6
- pair_target: int32 [2, 10240], P('dp', 'space'), may hold values from 0 to 3, as said below
- pair_source: int32 [2, 10240], P('dp', 'space'), may hold values from 0 to 7, as said below
- pair_count: int32 [2, 512], P('dp', 'space'), may hold values from 4 to 20, as said below
- radial_weight: float32 [8, 128], replicated, may hold values from -2 to 2
- mix_weight: bfloat16 [384, 128], replicated, may hold values from -0.3125 to 0.3125
- readout_weight: float32 [128], replicated, may hold values from -0.5 to 0.5
- species_shift: float32 [8], replicated, may hold values from -4 to 4
Outputs:
- atom_energy: float32 [2, 131072], P('dp', 'space')
- feature_grad: float32 [2, 128, 131072], P('dp', None, 'space')
- radial_grad: float32 [8, 128], replicated
- mix_grad: float32 [384, 128], replicated
- readout_grad: float32 [128], replicated
- shift_grad: float32 [8], replicated
The draws below stay inside these ranges and needn't reach their ends.
Inputs may be any that keep to these rules, and one draw needn't show every extreme that they name: `pair_target`: the target cell of a slot lies in its slab. `pair_source`: A live slot's source cell lies within 2 cells of its target cell and inside the snapshot; every target cell pairs with itself; no pair appears twice in a slab. `pair_count`: counts differ from slab to slab; in every snapshot some slab uses all 20 slots.
All inputs are finite; a program needn't handle non-finite values.
Results may differ from the reference program's by a relative error of at most 0.0009.
The reference program's roundings to bfloat16 on the way (of `scaled`, `factor`, `invariants`, `grad_pre` and `grad_msg`) count: a program that leaves them out, or rounds other values in their place, can miss the bound.
Values sent between devices are 32-bit elements; how exact they have to be, the bound alone decides.
A program may use at most 32 MiB of HBM per device.

```python
import math
import jax
import jax.numpy as jnp
from jax import lax

CH = 128
NB = 8
NSPEC = 8
CELL_ATOMS = 64
HALO_CELLS = 2
CELLS_DEV = 4
DOMAINS = 512
SNAPS = 2
MAXP = 20
PAIRS = 10240
ATOMS = 131072


cell_width = 2.5


def draw_positions(key, part):
    unit = jax.random.uniform(key, (SNAPS, 3, ATOMS), jnp.float32)
    cells = (jnp.arange(ATOMS).astype(jnp.int32) // CELL_ATOMS).astype(jnp.float32)
    across = math.sqrt(4.0 * CELL_ATOMS)
    along = (cells[None, :] + unit[:, 0]) * cell_width
    return jnp.stack([along, unit[:, 1] * across, unit[:, 2] * across], axis=1)


def pair_tables(key):
    base = jax.random.fold_in(key, 7)
    key_one, key_two, key_three = jax.random.split(base, 3)
    reach = 2 * HALO_CELLS + 1
    levels = jax.random.randint(key_one, (SNAPS, DOMAINS), 10, 101)
    dense = jax.random.randint(key_two, (SNAPS,), 1, DOMAINS - 1)
    domain = jnp.arange(DOMAINS).astype(jnp.int32)
    levels = jnp.where(domain[None, :] == dense[:, None], 101, levels)
    rolls = jax.random.randint(key_three, (SNAPS, DOMAINS, CELLS_DEV, reach), 0, 100)
    offsets = jnp.arange(reach).astype(jnp.int32) - HALO_CELLS
    cells = jnp.arange(CELLS_DEV).astype(jnp.int32)
    global_cell = domain[:, None, None] * CELLS_DEV + cells[None, :, None] + offsets[None, None, :]
    inside = (global_cell >= 0) & (global_cell < DOMAINS * CELLS_DEV)
    chosen = ((rolls < levels[:, :, None, None]) | (offsets[None, None, None, :] == 0)) & inside[None]
    chosen = chosen.reshape(SNAPS, DOMAINS, MAXP).astype(jnp.int32)
    source_value = (cells[:, None] + HALO_CELLS + offsets[None, :]).reshape(MAXP)
    target_value = jnp.broadcast_to(cells[:, None], (CELLS_DEV, reach)).reshape(MAXP)
    places = jnp.where(chosen > 0, jnp.cumsum(chosen, axis=-1) - 1, MAXP)
    counts = jnp.sum(chosen, axis=-1)
    onehot = (places[..., :, None] == jnp.arange(MAXP).astype(jnp.int32)).astype(jnp.int32)
    targets = jnp.sum(onehot * target_value[:, None], axis=-2)
    sources = jnp.sum(onehot * source_value[:, None], axis=-2)
    filled = jnp.arange(MAXP).astype(jnp.int32)[None, None, :] < counts[..., None]
    targets = jnp.where(filled, targets, 0)
    sources = jnp.where(filled, sources, HALO_CELLS)
    return (targets.reshape(SNAPS, PAIRS), sources.reshape(SNAPS, PAIRS), counts)


def draw_pair_target(key, part):
    return pair_tables(key)[0]


def draw_pair_source(key, part):
    return pair_tables(key)[1]


def draw_pair_count(key, part):
    return pair_tables(key)[2]


def plant(entries, stream_key, low, high):
    longest = entries.shape.index(max(entries.shape))
    spots = []
    for shift in (0, 1):
        where = [jax.random.randint(jax.random.fold_in(stream_key, axis), (), 0, length) for axis, length in enumerate(entries.shape)]
        where[longest] = (where[longest] + shift) % entries.shape[longest]
        spots.append(tuple(where))
    return entries.at[spots[0]].set(low).at[spots[1]].set(high)


def steps_of(key, shape, shards, least, high):
    level = 1.0
    for dim, parts in shards:
        draws = jax.random.uniform(jax.random.fold_in(jax.random.fold_in(key, 6), dim), (parts,), jnp.float32, least / len(shards), high / len(shards))
        level = level * jnp.repeat(jnp.exp(draws), shape[dim] // parts).reshape((-1,) + (1,) * (len(shape) - 1 - dim))
    return level


def normal_values(key, dims, spread, limit, cuts=(), kind=jnp.bfloat16):
    gain = steps_of(key, dims, cuts, -0.22, 0.18) if cuts else 1.0
    drawn = jax.random.normal(key, dims, jnp.float32) * spread * gain
    return jnp.minimum(jnp.maximum(drawn, -limit), limit).astype(kind)


def setup_inputs(seed: int = 0) -> dict:
    key_of = jax.random.split(jax.random.key(seed), 12)
    node_features = normal_values(key_of[0], (SNAPS, CH, ATOMS), 1.0, 6.0, ((0, 2), (2, 512)), jnp.float32)
    positions = draw_positions(jax.random.fold_in(key_of[11], 71), 0)
    species = plant(jax.random.randint(key_of[2], (SNAPS, ATOMS), 0, NSPEC), jax.random.fold_in(key_of[2], 1), 0, NSPEC - 1).astype(jnp.int32)
    energy_cotangent = normal_values(key_of[3], (SNAPS, ATOMS), 1.0, 6.0, ((0, 2), (1, 512)), jnp.float32)
    pair_target = draw_pair_target(jax.random.fold_in(key_of[11], 71), 0)
    pair_source = draw_pair_source(jax.random.fold_in(key_of[11], 71), 0)
    pair_count = draw_pair_count(jax.random.fold_in(key_of[11], 71), 0)
    radial_weight = normal_values(key_of[7], (NB, CH), 0.35, 2.0, (), jnp.float32)
    mix_weight = normal_values(key_of[8], (3 * CH, CH), (3 * CH) ** -0.5, 0.3125)
    readout_weight = normal_values(key_of[9], (CH,), CH ** -0.5, 0.5, (), jnp.float32)
    species_shift = normal_values(key_of[10], (NSPEC,), 1.0, 4.0, (), jnp.float32)
    return {"node_features": node_features, "positions": positions, "species": species, "energy_cotangent": energy_cotangent, "pair_target": pair_target, "pair_source": pair_source, "pair_count": pair_count, "radial_weight": radial_weight, "mix_weight": mix_weight, "readout_weight": readout_weight, "species_shift": species_shift}


cutoff = 5.0
message_scale = 0.25

def harmonics(delta):
    delta_x = delta[0]
    delta_y = delta[1]
    delta_z = delta[2]
    square_dist = delta_x * delta_x + delta_y * delta_y + delta_z * delta_z
    root_three = math.sqrt(3.0)
    root_fifteen = math.sqrt(15.0)
    root_five = math.sqrt(5.0)
    return jnp.stack([jnp.ones_like(delta_x), root_three * delta_x, root_three * delta_y, root_three * delta_z, root_fifteen * delta_x * delta_y, root_fifteen * delta_y * delta_z, 0.5 * root_five * (3.0 * delta_z * delta_z - square_dist), root_fifteen * delta_x * delta_z, 0.5 * root_fifteen * (delta_x * delta_x - delta_y * delta_y)])

def edge_table(target_coords, source_coords, self_block):
    delta = (target_coords[:, :, None] - source_coords[:, None, :]) / cutoff
    square_dist = lax.optimization_barrier(jnp.sum(delta * delta, axis=0))
    distance = jnp.sqrt(square_dist)
    envelope = jnp.square(jnp.maximum(1.0 - square_dist, 0.0))
    envelope = envelope * (1.0 - self_block * jnp.eye(CELL_ATOMS, dtype=jnp.float32))
    orders = jnp.arange(1, NB + 1).astype(jnp.float32)
    radial = jnp.sinc(orders[:, None, None] * distance[None]) * envelope[None] * message_scale
    harmonic = harmonics(delta)
    radial_t = jnp.transpose(radial, (0, 2, 1))
    harmonic_t = jnp.transpose(harmonic, (2, 0, 1))
    factor = radial_t[:, :, None, :] * harmonic_t[None]
    return factor.reshape(NB * CELL_ATOMS, 9 * CELL_ATOMS).astype(jnp.bfloat16)

def keep_same(values):
    return values

def snapshot_step(features, coords, kinds, energy_grad, targets, sources, counts, radial_weight, mix_weight, readout_weight, species_shift):
    slot = jnp.arange(PAIRS).astype(jnp.int32)
    domain = slot // MAXP
    target_cell = domain * CELLS_DEV + targets
    source_cell = domain * CELLS_DEV + sources - HALO_CELLS
    usable = slot % MAXP < counts[domain]
    scaled = (features[:, None, :] * radial_weight.T[:, :, None]).astype(jnp.bfloat16)

    def forward_step(totals, record):
        tcell, scell, live = record

        def add(current):
            tco = lax.dynamic_slice_in_dim(coords, tcell * CELL_ATOMS, CELL_ATOMS, 1)
            sco = lax.dynamic_slice_in_dim(coords, scell * CELL_ATOMS, CELL_ATOMS, 1)
            factor = edge_table(tco, sco, (tcell == scell).astype(jnp.float32))
            block = lax.dynamic_slice_in_dim(scaled, scell * CELL_ATOMS, CELL_ATOMS, 2).reshape(CH, NB * CELL_ATOMS)
            product = jnp.dot(block, factor, preferred_element_type=jnp.float32).reshape(CH, 9, CELL_ATOMS)
            before = lax.dynamic_slice_in_dim(current, tcell * CELL_ATOMS, CELL_ATOMS, 2)
            return lax.dynamic_update_slice_in_dim(current, before + product, tcell * CELL_ATOMS, 2)
        return (lax.cond(live, add, keep_same, totals), None)
    messages, unused = lax.scan(forward_step, jnp.zeros((CH, 9, ATOMS), jnp.float32), (target_cell, source_cell, usable))
    invariants = jnp.concatenate([messages[:, 0], 0.5 * lax.optimization_barrier(jnp.sum(messages[:, 1:4] ** 2, axis=1)), 0.5 * lax.optimization_barrier(jnp.sum(messages[:, 4:9] ** 2, axis=1))], axis=0).astype(jnp.bfloat16)
    preact = lax.dot_general(mix_weight, invariants, (((0,), (0,)), ((), ())), preferred_element_type=jnp.float32)
    gating = jax.nn.sigmoid(preact)
    updated = features + preact * gating
    onehot = (kinds[None, :] == jnp.arange(NSPEC).astype(jnp.int32)[:, None]).astype(jnp.float32)
    energy = lax.optimization_barrier(jnp.sum(updated * readout_weight[:, None], axis=0)) + lax.optimization_barrier(jnp.sum(onehot * species_shift[:, None], axis=0))
    grad_out = lax.optimization_barrier(jnp.sum(updated * energy_grad[None, :], axis=1))
    grad_shift = lax.optimization_barrier(jnp.sum(onehot * energy_grad[None, :], axis=1))
    grad_pre = (energy_grad[None, :] * readout_weight[:, None] * gating * (1.0 + preact * (1.0 - gating))).astype(jnp.bfloat16)
    grad_mix = lax.dot_general(invariants, grad_pre, (((1,), (1,)), ((), ())), preferred_element_type=jnp.float32)
    grad_inv = jnp.dot(mix_weight, grad_pre, preferred_element_type=jnp.float32)
    grad_msg = jnp.concatenate([grad_inv[:CH][:, None], grad_inv[CH:2 * CH][:, None] * messages[:, 1:4], grad_inv[2 * CH:][:, None] * messages[:, 4:9]], axis=1).astype(jnp.bfloat16)

    def backward_step(totals, record):
        tcell, scell, live = record

        def add(current):
            tco = lax.dynamic_slice_in_dim(coords, tcell * CELL_ATOMS, CELL_ATOMS, 1)
            sco = lax.dynamic_slice_in_dim(coords, scell * CELL_ATOMS, CELL_ATOMS, 1)
            factor = edge_table(tco, sco, (tcell == scell).astype(jnp.float32))
            block = lax.dynamic_slice_in_dim(grad_msg, tcell * CELL_ATOMS, CELL_ATOMS, 2).reshape(CH, 9 * CELL_ATOMS)
            product = lax.dot_general(block, factor, (((1,), (1,)), ((), ())), preferred_element_type=jnp.float32)
            before = lax.dynamic_slice_in_dim(current, scell * CELL_ATOMS, CELL_ATOMS, 2)
            return lax.dynamic_update_slice_in_dim(current, before + product.reshape(CH, NB, CELL_ATOMS), scell * CELL_ATOMS, 2)
        return (lax.cond(live, add, keep_same, totals), None)
    grad_scaled, unused = lax.scan(backward_step, jnp.zeros((CH, NB, ATOMS), jnp.float32), (target_cell, source_cell, usable))
    feature_grad = readout_weight[:, None] * energy_grad[None, :] + lax.optimization_barrier(jnp.sum(grad_scaled * radial_weight.T[:, :, None], axis=1))
    grad_radial = lax.optimization_barrier(jnp.sum(grad_scaled * features[:, None, :], axis=2)).T
    return (energy, feature_grad, grad_radial, grad_mix, grad_out, grad_shift)

def reference(node_features, positions, species, energy_cotangent, pair_target, pair_source, pair_count, radial_weight, mix_weight, readout_weight, species_shift):
    energies = []
    feature_grads = []
    radial_sum = jnp.zeros((NB, CH), jnp.float32)
    mix_sum = jnp.zeros((3 * CH, CH), jnp.float32)
    out_sum = jnp.zeros((CH,), jnp.float32)
    shift_sum = jnp.zeros((NSPEC,), jnp.float32)
    for snapshot in range(SNAPS):
        results = snapshot_step(node_features[snapshot], positions[snapshot], species[snapshot], energy_cotangent[snapshot], pair_target[snapshot], pair_source[snapshot], pair_count[snapshot], radial_weight, mix_weight, readout_weight, species_shift)
        energies.append(results[0])
        feature_grads.append(results[1])
        radial_sum = radial_sum + results[2]
        mix_sum = mix_sum + results[3]
        out_sum = out_sum + results[4]
        shift_sum = shift_sum + results[5]
    scale = 1.0 / math.sqrt(ATOMS * SNAPS)
    return (jnp.stack(energies), jnp.stack(feature_grads), radial_sum * scale, mix_sum * scale, out_sum * scale, shift_sum * scale)
```

```python
import functools
import math

import jax
import jax.numpy as jnp
from jax import lax
from jax.experimental import pallas as pl
from jax.experimental.pallas import tpu as pltpu
from jax.sharding import PartitionSpec as P

CH = 128
NB = 8
NY = 9
NSPEC = 8
CELL = 64
BLK = 128
F32 = jnp.float32
BF16 = jnp.bfloat16
MESH = pl.DeviceIdType.MESH

SPLIT = {"xh": 2, "z": 32, "zlo": 4, "y": 4, "core": 2}
ROWS = 512

COS_TERMS = [(-1.0) ** k * math.pi ** (2 * k) / math.factorial(2 * k) for k in range(11)]
SINC_TERMS = [(-1.0) ** k * math.pi ** (2 * k) / math.factorial(2 * k + 1) for k in range(10)]


def horner(terms, x):
    total = x * terms[-1] + terms[-2]
    for term in reversed(terms[:-2]):
        total = total * x + term
    return total


def nt_dot(a, b):
    return lax.dot_general(a, b, (((1,), (1,)), ((), ())), preferred_element_type=F32)


def nn_dot(a, b):
    return jnp.dot(a, b, preferred_element_type=F32)


def column(row):
    return jnp.transpose(jnp.broadcast_to(row, (BLK, BLK)))


def kernel(
    dims,
    feat_ref,
    pos_ref,
    spec_ref,
    eg_ref,
    pt_ref,
    ps_ref,
    pc_ref,
    w_ref,
    mix_ref,
    ro_ref,
    sh_ref,
    energy_ref,
    fgrad_ref,
    rad_ref,
    mixg_ref,
    rog_ref,
    shg_ref,
    table,
    scaled,
    feats,
    scol,
    wcol,
    live,
    msg,
    gmsg,
    inv,
    racc,
    gext,
    halo_out,
    halo_in,
    grad_in,
    big_src,
    big_rs,
    z_a,
    z_b,
    z_as,
    z_bs,
    big_ag,
    sm_src,
    sm_pl,
    sm_sum,
    sm_x,
    sm_z,
    send_sem,
    recv_sem,
):
    nsp, ndp, nxh, nz, zlo, ny, nco = dims
    plane = nxh * ndp * ny * nco
    zhi = nz // zlo
    sp = lax.axis_index("space")
    dp = lax.axis_index("dp")
    core = sp % nco
    yy = (sp // nco) % ny
    zz = (sp // (nco * ny)) % nz
    xh = sp // (nco * ny * nz)
    me = ((xh * ndp + dp) * ny + yy) * nco + core

    def at_plane(g):
        return (
            ((g // (nco * ny * ndp)) * nz + zz) * (ny * nco) + g % (nco * ny),
            (g // (nco * ny)) % ndp,
        )

    def at_z(z):
        return ((xh * nz + z) * ny + yy) * nco + core, dp

    def plane_peer(k):
        return (me + k) % plane

    def za_peer(k):
        return (zz // zlo) * zlo + (zz % zlo + k) % zlo

    def zb_peer(k):
        return ((zz // zlo + k) % zhi) * zlo + zz % zlo

    def remote(src, dst, n, dev):
        return pltpu.make_async_remote_copy(
            src_ref=src,
            dst_ref=dst,
            send_sem=send_sem.at[n],
            recv_sem=recv_sem.at[n],
            device_id=dev,
            device_id_type=MESH,
        )

    barrier = pltpu.get_barrier_semaphore()

    def greet(dev):
        pl.semaphore_signal(barrier, inc=1, device_id=dev, device_id_type=MESH)

    has_left = sp > 0
    has_right = sp < nsp - 1

    @pl.when(has_left)
    def _():
        greet((sp - 1, dp))

    @pl.when(has_right)
    def _():
        greet((sp + 1, dp))

    def greet_plane(k, c):
        greet(at_plane(plane_peer(k)))
        return c

    lax.fori_loop(1, plane, greet_plane, 0)
    for k in range(1, zlo):
        greet(at_z(za_peer(k)))
    for k in range(1, zhi):
        greet(at_z(zb_peer(k)))

    @pl.when(me > 0)
    def _():
        greet(at_z((zz + me) % nz))
        greet(at_z((zz + nz - me) % nz))

    features = feat_ref[0]
    for s in range(2):
        halo_out[s, 0:CH, :] = features[:, s * BLK : (s + 1) * BLK]
        halo_out[s, CH : CH + 3, :] = pos_ref[0, :, s * BLK : (s + 1) * BLK]
        halo_out[s, CH + 3 : CH + 8, :] = jnp.zeros((5, BLK), F32)
        feats[1 + s] = features[:, s * BLK : (s + 1) * BLK]
        for d in range(3):
            scol[1 + s, d] = column(pos_ref[0, d : d + 1, s * BLK : (s + 1) * BLK])

    for b in range(NB):
        wcol[b] = column(w_ref[b : b + 1, :])
    for s in range(2):
        for b in range(NB):
            scaled[1 + s, :, b * BLK : (b + 1) * BLK] = (feats[1 + s] * wcol[b]).astype(BF16)

    slots = pt_ref.shape[1]
    used = lax.broadcasted_iota(jnp.int32, (1, slots), 1) < pc_ref[...]
    hit_source = ps_ref[...] == lax.broadcasted_iota(jnp.int32, (8, slots), 0)
    lane = lax.broadcasted_iota(jnp.int32, (8, BLK), 1)
    for t in range(2):
        cols = []
        for h in range(2):
            hit = hit_source & (used & (pt_ref[...] == 2 * t + h))
            cols.append(jnp.sum(jnp.where(hit, 1.0, 0.0), axis=1, keepdims=True))
        live[t] = jnp.where(lane < CELL, cols[0], cols[1])

    msg[...] = jnp.zeros_like(msg)

    root3 = math.sqrt(3.0)
    root15 = math.sqrt(15.0)
    root5 = math.sqrt(5.0)
    sub16 = lax.broadcasted_iota(jnp.int32, (16, BLK), 0)
    lane16 = lax.broadcasted_iota(jnp.int32, (16, BLK), 1)

    def produce(p, t, s):
        lanes = pl.ds(pl.multiple_of(t * BLK, BLK), BLK)
        targets = [jnp.broadcast_to(pos_ref[0, d : d + 1, lanes], (16, BLK)) for d in range(3)]
        shift = jnp.where(s == t + 1, 0, 2 * BLK)

        def chunk(q, c):
            r0 = pl.multiple_of(q * 16, 16)
            rows = pl.ds(r0, 16)
            ux, uy, uz = [(targets[d] - scol[s, d, rows, :]) * 0.2 for d in range(3)]
            square = ux * ux + uy * uy + uz * uz
            alive = jnp.broadcast_to(live[t, pl.ds(2 * s + q // 4, 1), :], (16, BLK)) > 0.5
            keep = (square < 1.0) & alive & (sub16 + (r0 + shift) != lane16)
            square = jnp.where(keep, square, 1.0)
            ux = jnp.where(keep, ux, 0.0)
            uy = jnp.where(keep, uy, 0.0)
            uz = jnp.where(keep, uz, 0.0)
            cosine2 = 2.0 * horner(COS_TERMS, square)
            gap = 1.0 - square
            base = (gap * gap) * (0.25 * horner(SINC_TERMS, square))
            ux15 = root15 * ux
            harmonic = [
                None,
                root3 * ux,
                root3 * uy,
                root3 * uz,
                ux15 * uy,
                root15 * uy * uz,
                (0.5 * root5) * (3.0 * uz * uz - square),
                ux15 * uz,
                (0.5 * root15) * (ux * ux - uy * uy),
            ]
            older, newer = None, base
            for b in range(NB):
                radial = newer * (1.0 / (b + 1)) if b else newer
                at = pl.ds(b * BLK + r0, 16)
                for y in range(NY):
                    value = radial * harmonic[y] if y else radial
                    table[p, at, y * BLK : (y + 1) * BLK] = value.astype(BF16)
                following = cosine2 * newer - older if b else cosine2 * newer
                older, newer = newer, following
            return c

        lax.fori_loop(0, BLK // 16, chunk, 0)

    def forward(p, t, s):
        produce(p, t, s)
        msg[t] += nn_dot(scaled[s], table[p])

    forward(1, 0, 1)

    total = plane - 1 + (zlo - 1) + (zhi - 1)
    total = total + has_left.astype(jnp.int32) + has_right.astype(jnp.int32)
    total = total + 2 * (me > 0).astype(jnp.int32)
    pl.semaphore_wait(barrier, total)

    to_left = remote(halo_out.at[0], halo_in.at[1], 0, (sp - 1, dp))
    to_right = remote(halo_out.at[1], halo_in.at[0], 1, (sp + 1, dp))

    @pl.when(has_left)
    def _():
        to_left.start()

    @pl.when(has_right)
    def _():
        to_right.start()

    def inner(p, c):
        forward(p, (p - 1) // 2, 1 + (p - 1) % 2)
        return c

    lax.fori_loop(2, 5, inner, 0)

    @pl.when(has_left)
    def _():
        to_right.wait_recv()

    @pl.when(has_right)
    def _():
        to_left.wait_recv()

    @pl.when(jnp.logical_not(has_left))
    def _():
        halo_in[0] = jnp.zeros((CH + 8, BLK), F32)

    @pl.when(jnp.logical_not(has_right))
    def _():
        halo_in[1] = jnp.zeros((CH + 8, BLK), F32)

    for h, s in ((0, 0), (1, 3)):
        feats[s] = halo_in[h, 0:CH, :]
        for d in range(3):
            scol[s, d] = column(halo_in[h, CH + d : CH + d + 1, :])
        for b in range(NB):
            scaled[s, :, b * BLK : (b + 1) * BLK] = (feats[s] * wcol[b]).astype(BF16)

    def outer(h, c):
        forward(5 * h, h, 3 * h)
        return c

    lax.fori_loop(0, 2, outer, 0)

    mix = mix_ref[...]
    mix_t = jnp.concatenate(
        [jnp.transpose(mix[k * CH : (k + 1) * CH].astype(F32)) for k in range(3)], axis=1
    ).astype(BF16)
    ro_col = column(ro_ref[...])
    lane_ch = lax.broadcasted_iota(jnp.int32, (CH, BLK), 1)
    row_sp = lax.broadcasted_iota(jnp.int32, (NSPEC, BLK), 0)
    shift_col = jnp.transpose(jnp.broadcast_to(sh_ref[...], (NSPEC, NSPEC)))[:, 0:1]
    for t in range(2):
        lanes = slice(t * BLK, (t + 1) * BLK)
        inv[0:CH, lanes] = msg[t, :, 0:BLK].astype(BF16)
        for k, ys in ((1, range(1, 4)), (2, range(4, 9))):
            acc = None
            for y in ys:
                m = msg[t, :, y * BLK : (y + 1) * BLK]
                acc = m * m if acc is None else acc + m * m
            inv[k * CH : (k + 1) * CH, lanes] = (0.5 * acc).astype(BF16)
    mixg = jnp.zeros((3 * CH, CH), F32)
    rog = jnp.zeros((CH, BLK), F32)
    shg = jnp.zeros((NSPEC, BLK), F32)
    for t in range(2):
        lanes = slice(t * BLK, (t + 1) * BLK)
        invariants = inv[:, lanes]
        preact = nn_dot(mix_t, invariants)
        gate = 1.0 / (1.0 + jnp.exp(-preact))
        updated = feats[1 + t] + preact * gate
        eg = eg_ref[:, lanes]
        onehot = (spec_ref[:, lanes] == row_sp).astype(F32)
        energy_ref[:, lanes] = jnp.sum(updated * ro_col, axis=0, keepdims=True) + jnp.sum(
            onehot * shift_col, axis=0, keepdims=True
        )
        rog += updated * eg
        shg += onehot * eg
        base = eg * ro_col
        gext[1 + t] = base
        gpre = (base * gate * (1.0 + preact * (1.0 - gate))).astype(BF16)
        mixg += nt_dot(invariants, gpre)
        ginv = nn_dot(mix, gpre)
        gmsg[t, :, 0:BLK] = ginv[0:CH].astype(BF16)
        for y in range(1, NY):
            k = 1 if y < 4 else 2
            gmsg[t, :, y * BLK : (y + 1) * BLK] = (
                ginv[k * CH : (k + 1) * CH] * msg[t, :, y * BLK : (y + 1) * BLK]
            ).astype(BF16)

    per = ROWS // plane
    tail = jnp.concatenate(
        [
            jnp.sum(jnp.transpose(rog), axis=0, keepdims=True),
            jnp.zeros((7, BLK), F32),
            jnp.sum(jnp.transpose(jnp.concatenate([shg, jnp.zeros((CH - NSPEC, BLK), F32)], axis=0)), axis=0, keepdims=True),
            jnp.zeros((ROWS - 3 * CH - 9, BLK), F32),
        ],
        axis=0,
    )
    big_src[...] = jnp.concatenate([mixg, tail], axis=0).reshape(plane, per, CH)

    def send_plane(src, dst, n):
        def step(k, c):
            g = plane_peer(k)
            remote(src(g), dst, n, at_plane(g)).start()
            return c

        lax.fori_loop(1, plane, step, 0)

    def wait_slots(buf, n, count, dev):
        part = buf.at[pl.ds(0, count)]
        copies = remote(part, part, n, dev)
        return copies

    big_rs[me] = big_src[me]
    send_plane(lambda g: big_src.at[g], big_rs.at[me], 2)

    racc[...] = jnp.zeros_like(racc)

    def backward(s, parts):
        def step(n, c):
            rows = pl.ds(pl.multiple_of(n * 256, 256), 256)
            g = nt_dot(gmsg[parts[0][1]], table[parts[0][0], rows, :])
            for p, t in parts[1:]:
                g += nt_dot(gmsg[t], table[p, rows, :])
            here = feats[s]
            add = gext[s]
            for h in range(2):
                gb = g[:, h * BLK : (h + 1) * BLK]
                add += gb * wcol[2 * n + h]
                racc[2 * n + h] += gb * here
            gext[s] = add
            return c

        lax.fori_loop(0, NB // 2, step, 0)

    gext[0] = jnp.zeros((CH, BLK), F32)
    gext[3] = jnp.zeros((CH, BLK), F32)
    backward(0, [(0, 0)])
    backward(3, [(5, 1)])

    back_left = remote(gext.at[0], grad_in.at[1], 3, (sp - 1, dp))
    back_right = remote(gext.at[3], grad_in.at[0], 4, (sp + 1, dp))

    @pl.when(has_left)
    def _():
        back_left.start()

    @pl.when(has_right)
    def _():
        back_right.start()

    any_plane = at_plane(plane_peer(1))
    any_a = at_z(za_peer(1))
    any_b = at_z(zb_peer(1))

    wait_slots(big_rs, 2, plane - 1, any_plane).wait_recv()
    z_as[...] = jnp.sum(big_rs[...], axis=0)
    z_a[zz % zlo] = z_as[...]
    for k in range(1, zlo):
        remote(z_as, z_a.at[zz % zlo], 5, at_z(za_peer(k))).start()

    backward(1, [(1, 0), (3, 1)])

    wait_slots(z_a, 5, zlo - 1, any_a).wait_recv()
    z_bs[...] = jnp.sum(z_a[...], axis=0)
    z_b[zz // zlo] = z_bs[...]
    for k in range(1, zhi):
        remote(z_bs, z_b.at[zz // zlo], 6, at_z(zb_peer(k))).start()

    backward(2, [(2, 0), (4, 1)])

    sm_src[...] = jnp.concatenate(
        [jnp.sum(jnp.transpose(racc[b]), axis=0, keepdims=True) for b in range(NB)], axis=0
    )
    sm_pl[me] = sm_src[...]
    send_plane(lambda g: sm_src, sm_pl.at[me], 7)

    wait_slots(z_b, 6, zhi - 1, any_b).wait_recv()
    big_ag[me] = jnp.sum(z_b[...], axis=0)
    send_plane(lambda g: big_ag.at[me], big_ag.at[me], 8)

    wait_slots(sm_pl, 7, plane - 1, any_plane).wait_recv()
    sm_sum[...] = jnp.sum(sm_pl[...], axis=0)
    slot = (zz + me) % nz
    to_z = remote(sm_sum, sm_x, 9, at_z((zz + nz - me) % nz))

    @pl.when(me > 0)
    def _():
        to_z.start()
        to_z.wait_recv()

    @pl.when(me == 0)
    def _():
        sm_x[...] = sm_sum[...]

    sm_z[slot] = sm_x[...]
    send_plane(lambda g: sm_x, sm_z.at[slot], 10)

    @pl.when(has_left)
    def _():
        back_right.wait_recv()
        gext[1] += grad_in[0]

    @pl.when(has_right)
    def _():
        back_left.wait_recv()
        gext[2] += grad_in[1]

    for t in range(2):
        fgrad_ref[0, :, t * BLK : (t + 1) * BLK] = gext[1 + t]

    scale = 1.0 / math.sqrt(2 * BLK * nsp * ndp)
    wait_slots(big_ag, 8, plane - 1, any_plane).wait_recv()
    whole = big_ag[...].reshape(ROWS, CH) * scale
    mixg_ref[...] = whole[0 : 3 * CH]
    rog_ref[...] = whole[3 * CH : 3 * CH + 1]
    shg_ref[...] = whole[3 * CH + 8 : 3 * CH + 9, 0:NSPEC]

    wait_slots(sm_z, 10, plane - 1, any_plane).wait_recv()
    rad_ref[...] = jnp.sum(sm_z[...], axis=0) * scale

    @pl.when(has_left)
    def _():
        to_left.wait_send()
        back_left.wait_send()

    @pl.when(has_right)
    def _():
        to_right.wait_send()
        back_right.wait_send()

    @pl.when(me > 0)
    def _():
        to_z.wait_send()

    wait_slots(big_rs, 2, plane - 1, any_plane).wait_send()
    wait_slots(z_a, 5, zlo - 1, any_a).wait_send()
    wait_slots(z_b, 6, zhi - 1, any_b).wait_send()
    wait_slots(sm_pl, 7, plane - 1, any_plane).wait_send()
    wait_slots(big_ag, 8, plane - 1, any_plane).wait_send()
    wait_slots(sm_z, 10, plane - 1, any_plane).wait_send()


def body(
    dims,
    node_features,
    positions,
    species,
    energy_cotangent,
    pair_target,
    pair_source,
    pair_count,
    radial_weight,
    mix_weight,
    readout_weight,
    species_shift,
):
    nsp, ndp, nxh, nz, zlo, ny, nco = dims
    plane = nxh * ndp * ny * nco
    zhi = nz // zlo
    per = ROWS // plane
    atoms = 2 * BLK
    vmem = pl.BlockSpec(memory_space=pltpu.VMEM)
    outs = pl.pallas_call(
        functools.partial(kernel, dims),
        out_shape=(
            jax.ShapeDtypeStruct((1, atoms), F32),
            jax.ShapeDtypeStruct((1, CH, atoms), F32),
            jax.ShapeDtypeStruct((NB, CH), F32),
            jax.ShapeDtypeStruct((3 * CH, CH), F32),
            jax.ShapeDtypeStruct((1, CH), F32),
            jax.ShapeDtypeStruct((1, NSPEC), F32),
        ),
        in_specs=[vmem] * 11,
        out_specs=(vmem,) * 6,
        scratch_shapes=[
            pltpu.VMEM((6, NB * BLK, NY * BLK), BF16),
            pltpu.VMEM((4, CH, NB * BLK), BF16),
            pltpu.VMEM((4, CH, BLK), F32),
            pltpu.VMEM((4, 3, BLK, BLK), F32),
            pltpu.VMEM((NB, CH, BLK), F32),
            pltpu.VMEM((2, 8, BLK), F32),
            pltpu.VMEM((2, CH, NY * BLK), F32),
            pltpu.VMEM((2, CH, NY * BLK), BF16),
            pltpu.VMEM((3 * CH, atoms), BF16),
            pltpu.VMEM((NB, CH, BLK), F32),
            pltpu.VMEM((4, CH, BLK), F32),
            pltpu.VMEM((2, CH + 8, BLK), F32),
            pltpu.VMEM((2, CH + 8, BLK), F32),
            pltpu.VMEM((2, CH, BLK), F32),
            pltpu.VMEM((plane, per, CH), F32),
            pltpu.VMEM((plane, per, CH), F32),
            pltpu.VMEM((zlo, per, CH), F32),
            pltpu.VMEM((zhi, per, CH), F32),
            pltpu.VMEM((per, CH), F32),
            pltpu.VMEM((per, CH), F32),
            pltpu.VMEM((plane, per, CH), F32),
            pltpu.VMEM((NB, CH), F32),
            pltpu.VMEM((plane, NB, CH), F32),
            pltpu.VMEM((NB, CH), F32),
            pltpu.VMEM((NB, CH), F32),
            pltpu.VMEM((nz, NB, CH), F32),
            pltpu.SemaphoreType.DMA((11,)),
            pltpu.SemaphoreType.DMA((11,)),
        ],
        compiler_params=pltpu.CompilerParams(
            collective_id=0, has_side_effects=True, vmem_limit_bytes=48 << 20
        ),
    )(
        node_features,
        positions,
        species,
        energy_cotangent,
        pair_target,
        pair_source,
        pair_count,
        radial_weight,
        mix_weight,
        readout_weight.reshape(1, CH),
        species_shift.reshape(1, NSPEC),
    )
    energy, feature_grad, grad_radial, grad_mix, grad_out, grad_shift = outs
    return energy, feature_grad, grad_radial, grad_mix, grad_out.reshape(CH), grad_shift.reshape(NSPEC)


def solution(mesh):
    sizes = dict(mesh.shape)
    dims = (
        sizes["space"],
        sizes["dp"],
        SPLIT["xh"],
        SPLIT["z"],
        SPLIT["zlo"],
        SPLIT["y"],
        SPLIT["core"],
    )
    return jax.shard_map(
        functools.partial(body, dims),
        mesh=mesh,
        in_specs=(
            P("dp", None, "space"),
            P("dp", None, "space"),
            P("dp", "space"),
            P("dp", "space"),
            P("dp", "space"),
            P("dp", "space"),
            P("dp", "space"),
            P(),
            P(),
            P(),
            P(),
        ),
        out_specs=(P("dp", "space"), P("dp", None, "space"), P(), P(), P(), P()),
        check_vma=False,
    )
```

```python
import functools
import math

import jax
import jax.numpy as jnp
from jax import lax
from jax.experimental import pallas as pl
from jax.experimental.pallas import tpu as pltpu
from jax.sharding import PartitionSpec as P

CH = 128
NB = 8
NY = 9
NSPEC = 8
CELL = 64
BLK = 128
F32 = jnp.float32
BF16 = jnp.bfloat16
MESH = pl.DeviceIdType.MESH

SPLIT = {"xh": 2, "z": 32, "zlo": 4, "y": 4, "core": 2}
ROWS = 512

COS_TERMS = [(-1.0) ** k * math.pi ** (2 * k) / math.factorial(2 * k) for k in range(11)]
SINC_TERMS = [(-1.0) ** k * math.pi ** (2 * k) / math.factorial(2 * k + 1) for k in range(10)]


def horner(terms, x):
    total = x * terms[-1] + terms[-2]
    for term in reversed(terms[:-2]):
        total = total * x + term
    return total


def nt_dot(a, b):
    return lax.dot_general(a, b, (((1,), (1,)), ((), ())), preferred_element_type=F32)


def nn_dot(a, b):
    return jnp.dot(a, b, preferred_element_type=F32)


def column(row):
    return jnp.transpose(jnp.broadcast_to(row, (BLK, BLK)))


def halo_kernel(dims, feat_ref, pos_ref, hfeat_ref, hpos_ref, pos_out, send_sem, recv_sem):
    nsp = dims[0]
    sp = lax.axis_index("space")
    dp = lax.axis_index("dp")
    has_left = sp > 0
    has_right = sp < nsp - 1
    barrier = pltpu.get_barrier_semaphore()

    @pl.when(has_left)
    def _():
        pl.semaphore_signal(barrier, inc=1, device_id=(sp - 1, dp), device_id_type=MESH)

    @pl.when(has_right)
    def _():
        pl.semaphore_signal(barrier, inc=1, device_id=(sp + 1, dp), device_id_type=MESH)

    for s in range(2):
        pos_out[s, 0:3, :] = pos_ref[0, :, s * BLK : (s + 1) * BLK]
        pos_out[s, 3:8, :] = jnp.zeros((5, BLK), F32)
    pl.semaphore_wait(barrier, has_left.astype(jnp.int32) + has_right.astype(jnp.int32))

    def copies(s, dev):
        return [
            pltpu.make_async_remote_copy(
                src_ref=src,
                dst_ref=dst,
                send_sem=send_sem.at[n],
                recv_sem=recv_sem.at[n],
                device_id=dev,
                device_id_type=MESH,
            )
            for n, src, dst in (
                (2 * s, feat_ref.at[0, :, pl.ds(s * BLK, BLK)], hfeat_ref.at[1 - s]),
                (2 * s + 1, pos_out.at[s], hpos_ref.at[1 - s]),
            )
        ]

    to_left = copies(0, (sp - 1, dp))
    to_right = copies(1, (sp + 1, dp))

    @pl.when(has_left)
    def _():
        for copy in to_left:
            copy.start()

    @pl.when(has_right)
    def _():
        for copy in to_right:
            copy.start()

    @pl.when(has_left)
    def _():
        for copy in to_right:
            copy.wait_recv()

    @pl.when(has_right)
    def _():
        for copy in to_left:
            copy.wait_recv()

    @pl.when(jnp.logical_not(has_left))
    def _():
        hfeat_ref[0] = jnp.zeros((CH, BLK), F32)
        hpos_ref[0] = jnp.zeros((8, BLK), F32)

    @pl.when(jnp.logical_not(has_right))
    def _():
        hfeat_ref[1] = jnp.zeros((CH, BLK), F32)
        hpos_ref[1] = jnp.zeros((8, BLK), F32)

    @pl.when(has_left)
    def _():
        for copy in to_left:
            copy.wait_send()

    @pl.when(has_right)
    def _():
        for copy in to_right:
            copy.wait_send()


def kernel(
    dims,
    feat_ref,
    pos_ref,
    hfeat_ref,
    hpos_ref,
    spec_ref,
    eg_ref,
    pt_ref,
    ps_ref,
    pc_ref,
    w_ref,
    mix_ref,
    ro_ref,
    sh_ref,
    energy_ref,
    fgrad_ref,
    rad_ref,
    mixg_ref,
    rog_ref,
    shg_ref,
    table,
    scaled,
    feats,
    scol,
    wcol,
    live,
    msg,
    gmsg,
    inv,
    racc,
    gext,
    grad_in,
    big_src,
    big_rs,
    z_a,
    z_b,
    z_as,
    z_bs,
    big_ag,
    sm_src,
    sm_pl,
    sm_sum,
    sm_x,
    sm_z,
    send_sem,
    recv_sem,
):
    nsp, ndp, nxh, nz, zlo, ny, nco = dims
    plane = nxh * ndp * ny * nco
    zhi = nz // zlo
    sp = lax.axis_index("space")
    dp = lax.axis_index("dp")
    core = sp % nco
    yy = (sp // nco) % ny
    zz = (sp // (nco * ny)) % nz
    xh = sp // (nco * ny * nz)
    me = ((xh * ndp + dp) * ny + yy) * nco + core

    def at_plane(g):
        return (
            ((g // (nco * ny * ndp)) * nz + zz) * (ny * nco) + g % (nco * ny),
            (g // (nco * ny)) % ndp,
        )

    def at_z(z):
        return ((xh * nz + z) * ny + yy) * nco + core, dp

    def plane_peer(k):
        return (me + k) % plane

    def za_peer(k):
        return (zz // zlo) * zlo + (zz % zlo + k) % zlo

    def zb_peer(k):
        return ((zz // zlo + k) % zhi) * zlo + zz % zlo

    def remote(src, dst, n, dev):
        return pltpu.make_async_remote_copy(
            src_ref=src,
            dst_ref=dst,
            send_sem=send_sem.at[n],
            recv_sem=recv_sem.at[n],
            device_id=dev,
            device_id_type=MESH,
        )

    barrier = pltpu.get_barrier_semaphore()

    def greet(dev):
        pl.semaphore_signal(barrier, inc=1, device_id=dev, device_id_type=MESH)

    has_left = sp > 0
    has_right = sp < nsp - 1

    @pl.when(has_left)
    def _():
        greet((sp - 1, dp))

    @pl.when(has_right)
    def _():
        greet((sp + 1, dp))

    def greet_plane(k, c):
        greet(at_plane(plane_peer(k)))
        return c

    lax.fori_loop(1, plane, greet_plane, 0)
    for k in range(1, zlo):
        greet(at_z(za_peer(k)))
    for k in range(1, zhi):
        greet(at_z(zb_peer(k)))

    @pl.when(me > 0)
    def _():
        greet(at_z((zz + me) % nz))
        greet(at_z((zz + nz - me) % nz))

    features = feat_ref[0]
    for s in range(2):
        feats[1 + s] = features[:, s * BLK : (s + 1) * BLK]
        for d in range(3):
            scol[1 + s, d] = column(pos_ref[0, d : d + 1, s * BLK : (s + 1) * BLK])

    for h, s in ((0, 0), (1, 3)):
        feats[s] = hfeat_ref[h]
        for d in range(3):
            scol[s, d] = column(hpos_ref[h, d : d + 1, :])
    for b in range(NB):
        wcol[b] = column(w_ref[b : b + 1, :])
    for s in range(4):
        for b in range(NB):
            scaled[s, :, b * BLK : (b + 1) * BLK] = (feats[s] * wcol[b]).astype(BF16)

    slots = pt_ref.shape[1]
    used = lax.broadcasted_iota(jnp.int32, (1, slots), 1) < pc_ref[...]
    hit_source = ps_ref[...] == lax.broadcasted_iota(jnp.int32, (8, slots), 0)
    lane = lax.broadcasted_iota(jnp.int32, (8, BLK), 1)
    for t in range(2):
        cols = []
        for h in range(2):
            hit = hit_source & (used & (pt_ref[...] == 2 * t + h))
            cols.append(jnp.sum(jnp.where(hit, 1.0, 0.0), axis=1, keepdims=True))
        live[t] = jnp.where(lane < CELL, cols[0], cols[1])

    root3 = math.sqrt(3.0)
    root15 = math.sqrt(15.0)
    root5 = math.sqrt(5.0)
    sub16 = lax.broadcasted_iota(jnp.int32, (16, BLK), 0)
    lane16 = lax.broadcasted_iota(jnp.int32, (16, BLK), 1)

    def produce(p, t, s):
        lanes = pl.ds(pl.multiple_of(t * BLK, BLK), BLK)
        targets = [jnp.broadcast_to(pos_ref[0, d : d + 1, lanes], (16, BLK)) for d in range(3)]
        shift = jnp.where(s == t + 1, 0, 2 * BLK)

        def chunk(q, c):
            r0 = pl.multiple_of(q * 16, 16)
            rows = pl.ds(r0, 16)
            ux, uy, uz = [(targets[d] - scol[s, d, rows, :]) * 0.2 for d in range(3)]
            square = ux * ux + uy * uy + uz * uz
            alive = jnp.broadcast_to(live[t, pl.ds(2 * s + q // 4, 1), :], (16, BLK)) > 0.5
            keep = (square < 1.0) & alive & (sub16 + (r0 + shift) != lane16)
            square = jnp.where(keep, square, 1.0)
            ux = jnp.where(keep, ux, 0.0)
            uy = jnp.where(keep, uy, 0.0)
            uz = jnp.where(keep, uz, 0.0)
            cosine2 = 2.0 * horner(COS_TERMS, square)
            gap = 1.0 - square
            base = (gap * gap) * (0.25 * horner(SINC_TERMS, square))
            ux15 = root15 * ux
            harmonic = [
                None,
                root3 * ux,
                root3 * uy,
                root3 * uz,
                ux15 * uy,
                root15 * uy * uz,
                (0.5 * root5) * (3.0 * uz * uz - square),
                ux15 * uz,
                (0.5 * root15) * (ux * ux - uy * uy),
            ]
            older, newer = None, base
            for b in range(NB):
                radial = newer * (1.0 / (b + 1)) if b else newer
                at = pl.ds(b * BLK + r0, 16)
                for y in range(NY):
                    value = radial * harmonic[y] if y else radial
                    table[p, at, y * BLK : (y + 1) * BLK] = value.astype(BF16)
                following = cosine2 * newer - older if b else cosine2 * newer
                older, newer = newer, following
            return c

        lax.fori_loop(0, BLK // 16, chunk, 0, unroll=True)

    def forward(p, c):
        t = p // 3
        produce(p, t, t + p % 3)
        return c

    lax.fori_loop(0, 6, forward, 0)
    for t in range(2):
        total = nn_dot(scaled[t], table[3 * t])
        for k in range(1, 3):
            total += nn_dot(scaled[t + k], table[3 * t + k])
        msg[t] = total

    mix = mix_ref[...]
    mix_t = jnp.concatenate(
        [jnp.transpose(mix[k * CH : (k + 1) * CH].astype(F32)) for k in range(3)], axis=1
    ).astype(BF16)
    ro_col = column(ro_ref[...])
    lane_ch = lax.broadcasted_iota(jnp.int32, (CH, BLK), 1)
    row_sp = lax.broadcasted_iota(jnp.int32, (NSPEC, BLK), 0)
    shift_col = jnp.transpose(jnp.broadcast_to(sh_ref[...], (NSPEC, NSPEC)))[:, 0:1]
    for t in range(2):
        lanes = slice(t * BLK, (t + 1) * BLK)
        inv[0:CH, lanes] = msg[t, :, 0:BLK].astype(BF16)
        for k, ys in ((1, range(1, 4)), (2, range(4, 9))):
            acc = None
            for y in ys:
                m = msg[t, :, y * BLK : (y + 1) * BLK]
                acc = m * m if acc is None else acc + m * m
            inv[k * CH : (k + 1) * CH, lanes] = (0.5 * acc).astype(BF16)
    mixg = jnp.zeros((3 * CH, CH), F32)
    rog = jnp.zeros((CH, BLK), F32)
    shg = jnp.zeros((NSPEC, BLK), F32)
    for t in range(2):
        lanes = slice(t * BLK, (t + 1) * BLK)
        invariants = inv[:, lanes]
        preact = nn_dot(mix_t, invariants)
        gate = 1.0 / (1.0 + jnp.exp(-preact))
        updated = feats[1 + t] + preact * gate
        eg = eg_ref[:, lanes]
        onehot = (spec_ref[:, lanes] == row_sp).astype(F32)
        energy_ref[:, lanes] = jnp.sum(updated * ro_col, axis=0, keepdims=True) + jnp.sum(
            onehot * shift_col, axis=0, keepdims=True
        )
        rog += updated * eg
        shg += onehot * eg
        base = eg * ro_col
        gext[1 + t] = base
        gpre = (base * gate * (1.0 + preact * (1.0 - gate))).astype(BF16)
        mixg += nt_dot(invariants, gpre)
        ginv = nn_dot(mix, gpre)
        gmsg[t, :, 0:BLK] = ginv[0:CH].astype(BF16)
        for y in range(1, NY):
            k = 1 if y < 4 else 2
            gmsg[t, :, y * BLK : (y + 1) * BLK] = (
                ginv[k * CH : (k + 1) * CH] * msg[t, :, y * BLK : (y + 1) * BLK]
            ).astype(BF16)

    per = ROWS // plane
    tail = jnp.concatenate(
        [
            jnp.sum(jnp.transpose(rog), axis=0, keepdims=True),
            jnp.zeros((7, BLK), F32),
            jnp.sum(jnp.transpose(jnp.concatenate([shg, jnp.zeros((CH - NSPEC, BLK), F32)], axis=0)), axis=0, keepdims=True),
            jnp.zeros((ROWS - 3 * CH - 9, BLK), F32),
        ],
        axis=0,
    )
    big_src[...] = jnp.concatenate([mixg, tail], axis=0).reshape(plane, per, CH)

    def send_plane(src, dst, n):
        def step(k, c):
            g = plane_peer(k)
            remote(src(g), dst, n, at_plane(g)).start()
            return c

        lax.fori_loop(1, plane, step, 0)

    def wait_slots(buf, n, count, dev):
        part = buf.at[pl.ds(0, count)]
        copies = remote(part, part, n, dev)
        return copies

    total = plane - 1 + (zlo - 1) + (zhi - 1)
    total = total + has_left.astype(jnp.int32) + has_right.astype(jnp.int32)
    total = total + 2 * (me > 0).astype(jnp.int32)
    pl.semaphore_wait(barrier, total)

    big_rs[me] = big_src[me]
    send_plane(lambda g: big_src.at[g], big_rs.at[me], 2)

    racc[...] = jnp.zeros_like(racc)

    def backward(s, parts):
        def step(n, c):
            rows = pl.ds(pl.multiple_of(n * 256, 256), 256)
            g = nt_dot(gmsg[parts[0][1]], table[parts[0][0], rows, :])
            for p, t in parts[1:]:
                g += nt_dot(gmsg[t], table[p, rows, :])
            here = feats[s]
            add = gext[s]
            for h in range(2):
                gb = g[:, h * BLK : (h + 1) * BLK]
                add += gb * wcol[2 * n + h]
                racc[2 * n + h] += gb * here
            gext[s] = add
            return c

        lax.fori_loop(0, NB // 2, step, 0, unroll=True)

    gext[0] = jnp.zeros((CH, BLK), F32)
    gext[3] = jnp.zeros((CH, BLK), F32)
    backward(0, [(0, 0)])
    backward(3, [(5, 1)])

    back_left = remote(gext.at[0], grad_in.at[1], 3, (sp - 1, dp))
    back_right = remote(gext.at[3], grad_in.at[0], 4, (sp + 1, dp))

    @pl.when(has_left)
    def _():
        back_left.start()

    @pl.when(has_right)
    def _():
        back_right.start()

    any_plane = at_plane(plane_peer(1))
    any_a = at_z(za_peer(1))
    any_b = at_z(zb_peer(1))

    wait_slots(big_rs, 2, plane - 1, any_plane).wait_recv()
    z_as[...] = jnp.sum(big_rs[...], axis=0)
    z_a[zz % zlo] = z_as[...]
    for k in range(1, zlo):
        remote(z_as, z_a.at[zz % zlo], 5, at_z(za_peer(k))).start()

    backward(1, [(1, 0), (3, 1)])

    wait_slots(z_a, 5, zlo - 1, any_a).wait_recv()
    z_bs[...] = jnp.sum(z_a[...], axis=0)
    z_b[zz // zlo] = z_bs[...]
    for k in range(1, zhi):
        remote(z_bs, z_b.at[zz // zlo], 6, at_z(zb_peer(k))).start()

    backward(2, [(2, 0), (4, 1)])

    sm_src[...] = jnp.concatenate(
        [jnp.sum(jnp.transpose(racc[b]), axis=0, keepdims=True) for b in range(NB)], axis=0
    )
    sm_pl[me] = sm_src[...]
    send_plane(lambda g: sm_src, sm_pl.at[me], 7)

    wait_slots(z_b, 6, zhi - 1, any_b).wait_recv()
    big_ag[me] = jnp.sum(z_b[...], axis=0)
    send_plane(lambda g: big_ag.at[me], big_ag.at[me], 8)

    wait_slots(sm_pl, 7, plane - 1, any_plane).wait_recv()
    sm_sum[...] = jnp.sum(sm_pl[...], axis=0)
    slot = (zz + me) % nz
    to_z = remote(sm_sum, sm_x, 9, at_z((zz + nz - me) % nz))

    @pl.when(me > 0)
    def _():
        to_z.start()
        to_z.wait_recv()

    @pl.when(me == 0)
    def _():
        sm_x[...] = sm_sum[...]

    sm_z[slot] = sm_x[...]
    send_plane(lambda g: sm_x, sm_z.at[slot], 10)

    @pl.when(has_left)
    def _():
        back_right.wait_recv()
        gext[1] += grad_in[0]

    @pl.when(has_right)
    def _():
        back_left.wait_recv()
        gext[2] += grad_in[1]

    for t in range(2):
        fgrad_ref[0, :, t * BLK : (t + 1) * BLK] = gext[1 + t]

    scale = 1.0 / math.sqrt(2 * BLK * nsp * ndp)
    wait_slots(big_ag, 8, plane - 1, any_plane).wait_recv()
    whole = big_ag[...].reshape(ROWS, CH) * scale
    mixg_ref[...] = whole[0 : 3 * CH]
    rog_ref[...] = whole[3 * CH : 3 * CH + 1]
    shg_ref[...] = whole[3 * CH + 8 : 3 * CH + 9, 0:NSPEC]

    wait_slots(sm_z, 10, plane - 1, any_plane).wait_recv()
    rad_ref[...] = jnp.sum(sm_z[...], axis=0) * scale

    @pl.when(has_left)
    def _():
        back_left.wait_send()

    @pl.when(has_right)
    def _():
        back_right.wait_send()

    @pl.when(me > 0)
    def _():
        to_z.wait_send()

    wait_slots(big_rs, 2, plane - 1, any_plane).wait_send()
    wait_slots(z_a, 5, zlo - 1, any_a).wait_send()
    wait_slots(z_b, 6, zhi - 1, any_b).wait_send()
    wait_slots(sm_pl, 7, plane - 1, any_plane).wait_send()
    wait_slots(big_ag, 8, plane - 1, any_plane).wait_send()
    wait_slots(sm_z, 10, plane - 1, any_plane).wait_send()


def body(
    dims,
    node_features,
    positions,
    species,
    energy_cotangent,
    pair_target,
    pair_source,
    pair_count,
    radial_weight,
    mix_weight,
    readout_weight,
    species_shift,
):
    nsp, ndp, nxh, nz, zlo, ny, nco = dims
    plane = nxh * ndp * ny * nco
    zhi = nz // zlo
    per = ROWS // plane
    atoms = 2 * BLK
    vmem = pl.BlockSpec(memory_space=pltpu.VMEM)
    halo_features, halo_positions = pl.pallas_call(
        functools.partial(halo_kernel, dims),
        out_shape=(
            jax.ShapeDtypeStruct((2, CH, BLK), F32),
            jax.ShapeDtypeStruct((2, 8, BLK), F32),
        ),
        in_specs=[vmem] * 2,
        out_specs=(vmem,) * 2,
        scratch_shapes=[
            pltpu.VMEM((2, 8, BLK), F32),
            pltpu.SemaphoreType.DMA((4,)),
            pltpu.SemaphoreType.DMA((4,)),
        ],
        compiler_params=pltpu.CompilerParams(collective_id=1, has_side_effects=True),
    )(node_features, positions)
    outs = pl.pallas_call(
        functools.partial(kernel, dims),
        out_shape=(
            jax.ShapeDtypeStruct((1, atoms), F32),
            jax.ShapeDtypeStruct((1, CH, atoms), F32),
            jax.ShapeDtypeStruct((NB, CH), F32),
            jax.ShapeDtypeStruct((3 * CH, CH), F32),
            jax.ShapeDtypeStruct((1, CH), F32),
            jax.ShapeDtypeStruct((1, NSPEC), F32),
        ),
        in_specs=[vmem] * 13,
        out_specs=(vmem,) * 6,
        scratch_shapes=[
            pltpu.VMEM((6, NB * BLK, NY * BLK), BF16),
            pltpu.VMEM((4, CH, NB * BLK), BF16),
            pltpu.VMEM((4, CH, BLK), F32),
            pltpu.VMEM((4, 3, BLK, BLK), F32),
            pltpu.VMEM((NB, CH, BLK), F32),
            pltpu.VMEM((2, 8, BLK), F32),
            pltpu.VMEM((2, CH, NY * BLK), F32),
            pltpu.VMEM((2, CH, NY * BLK), BF16),
            pltpu.VMEM((3 * CH, atoms), BF16),
            pltpu.VMEM((NB, CH, BLK), F32),
            pltpu.VMEM((4, CH, BLK), F32),
            pltpu.VMEM((2, CH, BLK), F32),
            pltpu.VMEM((plane, per, CH), F32),
            pltpu.VMEM((plane, per, CH), F32),
            pltpu.VMEM((zlo, per, CH), F32),
            pltpu.VMEM((zhi, per, CH), F32),
            pltpu.VMEM((per, CH), F32),
            pltpu.VMEM((per, CH), F32),
            pltpu.VMEM((plane, per, CH), F32),
            pltpu.VMEM((NB, CH), F32),
            pltpu.VMEM((plane, NB, CH), F32),
            pltpu.VMEM((NB, CH), F32),
            pltpu.VMEM((NB, CH), F32),
            pltpu.VMEM((nz, NB, CH), F32),
            pltpu.SemaphoreType.DMA((11,)),
            pltpu.SemaphoreType.DMA((11,)),
        ],
        compiler_params=pltpu.CompilerParams(
            collective_id=0, has_side_effects=True, vmem_limit_bytes=48 << 20
        ),
    )(
        node_features,
        positions,
        halo_features,
        halo_positions,
        species,
        energy_cotangent,
        pair_target,
        pair_source,
        pair_count,
        radial_weight,
        mix_weight,
        readout_weight.reshape(1, CH),
        species_shift.reshape(1, NSPEC),
    )
    energy, feature_grad, grad_radial, grad_mix, grad_out, grad_shift = outs
    return energy, feature_grad, grad_radial, grad_mix, grad_out.reshape(CH), grad_shift.reshape(NSPEC)


def solution(mesh):
    sizes = dict(mesh.shape)
    dims = (
        sizes["space"],
        sizes["dp"],
        SPLIT["xh"],
        SPLIT["z"],
        SPLIT["zlo"],
        SPLIT["y"],
        SPLIT["core"],
    )
    return jax.shard_map(
        functools.partial(body, dims),
        mesh=mesh,
        in_specs=(
            P("dp", None, "space"),
            P("dp", None, "space"),
            P("dp", "space"),
            P("dp", "space"),
            P("dp", "space"),
            P("dp", "space"),
            P("dp", "space"),
            P(),
            P(),
            P(),
            P(),
        ),
        out_specs=(P("dp", "space"), P("dp", None, "space"), P(), P(), P(), P()),
        check_vma=False,
    )
```

```python
import functools
import math

import jax
import jax.numpy as jnp
from jax import lax
from jax.experimental import pallas as pl
from jax.experimental.pallas import tpu as pltpu
from jax.sharding import PartitionSpec as P

CH = 128
NB = 8
NY = 9
NSPEC = 8
CELL = 64
BLK = 128
F32 = jnp.float32
BF16 = jnp.bfloat16
MESH = pl.DeviceIdType.MESH

SPLIT = {"xh": 2, "z": 32, "zlo": 4, "y": 4, "core": 2}

COS_TERMS = [(-1.0) ** k * math.pi ** (2 * k) / math.factorial(2 * k) for k in range(11)]
SINC_TERMS = [(-1.0) ** k * math.pi ** (2 * k) / math.factorial(2 * k + 1) for k in range(10)]


def horner(terms, x):
    total = x * terms[-1] + terms[-2]
    for term in reversed(terms[:-2]):
        total = total * x + term
    return total


def nt_dot(a, b):
    return lax.dot_general(a, b, (((1,), (1,)), ((), ())), preferred_element_type=F32)


def nn_dot(a, b):
    return jnp.dot(a, b, preferred_element_type=F32)


def column(row):
    return jnp.transpose(jnp.broadcast_to(row, (BLK, BLK)))


def store_all(*refs):
    sources, targets, sem = refs[:6], refs[6:12], refs[12]
    copies = [pltpu.make_async_copy(s, t, sem.at[n]) for n, (s, t) in enumerate(zip(sources, targets))]
    for copy in copies:
        copy.start()
    for copy in copies:
        copy.wait()


def kernel(
    dims,
    feat_hbm,
    pos_hbm,
    spec_hbm,
    eg_hbm,
    pt_hbm,
    ps_hbm,
    pc_hbm,
    w_hbm,
    mix_hbm,
    ro_hbm,
    sh_hbm,
    energy_hbm,
    fgrad_hbm,
    rad_hbm,
    mixg_hbm,
    rog_hbm,
    shg_hbm,
    table,
    scaled,
    feats,
    scol,
    wcol,
    live,
    msg,
    gmsg,
    inv,
    upd,
    gpre,
    racc,
    gext,
    halo_out,
    halo_in,
    grad_in,
    big_src,
    big_rs,
    z_a,
    z_b,
    z_as,
    z_bs,
    big_ag,
    sm_src,
    sm_pl,
    sm_sum,
    sm_x,
    sm_z,
    feat_ref,
    pos_ref,
    spec_ref,
    eg_ref,
    pt_ref,
    ps_ref,
    pc_ref,
    w_ref,
    mix_ref,
    ro_ref,
    sh_ref,
    energy_ref,
    fgrad_ref,
    rad_ref,
    mixg_ref,
    rog_ref,
    shg_ref,
    in_sem,
    out_sem,
    send_sem,
    recv_sem,
):
    nsp, ndp, nxh, nz, zlo, ny, nco = dims
    plane = nxh * ndp * ny * nco
    zhi = nz // zlo
    sp = lax.axis_index("space")
    dp = lax.axis_index("dp")
    core = sp % nco
    yy = (sp // nco) % ny
    zz = (sp // (nco * ny)) % nz
    xh = sp // (nco * ny * nz)
    me = ((xh * ndp + dp) * ny + yy) * nco + core

    def at_plane(g):
        return (
            ((g // (nco * ny * ndp)) * nz + zz) * (ny * nco) + g % (nco * ny),
            (g // (nco * ny)) % ndp,
        )

    def at_z(z):
        return ((xh * nz + z) * ny + yy) * nco + core, dp

    def plane_peer(k):
        return (me + k) % plane

    def za_peer(k):
        return (zz // zlo) * zlo + (zz % zlo + k) % zlo

    def zb_peer(k):
        return ((zz // zlo + k) % zhi) * zlo + zz % zlo

    def remote(src, dst, n, dev):
        return pltpu.make_async_remote_copy(
            src_ref=src,
            dst_ref=dst,
            send_sem=send_sem.at[n],
            recv_sem=recv_sem.at[n],
            device_id=dev,
            device_id_type=MESH,
        )

    fetches = [
        pltpu.make_async_copy(src, dst, in_sem.at[n])
        for n, (src, dst) in enumerate(
            (
                (feat_hbm, feat_ref),
                (pos_hbm, pos_ref),
                (pt_hbm, pt_ref),
                (ps_hbm, ps_ref),
                (pc_hbm, pc_ref),
                (w_hbm, w_ref),
                (eg_hbm, eg_ref),
                (spec_hbm, spec_ref),
                (mix_hbm, mix_ref),
                (ro_hbm, ro_ref),
                (sh_hbm, sh_ref),
            )
        )
    ]
    for fetch in fetches:
        fetch.start()
    stores = [
        pltpu.make_async_copy(src, dst, out_sem.at[n])
        for n, (src, dst) in enumerate(
            (
                (energy_ref, energy_hbm),
                (fgrad_ref, fgrad_hbm),
                (rad_ref, rad_hbm),
                (mixg_ref, mixg_hbm),
                (rog_ref, rog_hbm),
                (shg_ref, shg_hbm),
            )
        )
    ]

    barrier = pltpu.get_barrier_semaphore()

    def greet(dev):
        pl.semaphore_signal(barrier, inc=1, device_id=dev, device_id_type=MESH)

    has_left = sp > 0
    has_right = sp < nsp - 1

    @pl.when(has_left)
    def _():
        greet((sp - 1, dp))

    @pl.when(has_right)
    def _():
        greet((sp + 1, dp))

    def greet_plane(k, c):
        greet(at_plane(plane_peer(k)))
        return c

    lax.fori_loop(1, plane, greet_plane, 0)
    for k in range(1, zlo):
        greet(at_z(za_peer(k)))
    for k in range(1, zhi):
        greet(at_z(zb_peer(k)))

    @pl.when(me > 0)
    def _():
        greet(at_z((zz + me) % nz))
        greet(at_z((zz + nz - me) % nz))

    for fetch in fetches[:6]:
        fetch.wait()
    features = feat_ref[0]
    for s in range(2):
        halo_out[s, 0:CH, :] = features[:, s * BLK : (s + 1) * BLK]
        for d in range(3):
            halo_out[s, CH + d : CH + d + 1, :] = pos_ref[d, :, s * BLK : (s + 1) * BLK]
        halo_out[s, CH + 3 : CH + 8, :] = jnp.zeros((5, BLK), F32)
        feats[1 + s] = features[:, s * BLK : (s + 1) * BLK]
        for d in range(3):
            scol[1 + s, d] = column(pos_ref[d, :, s * BLK : (s + 1) * BLK])

    for b in range(NB):
        wcol[b] = column(w_ref[b : b + 1, :])
    for s in range(2):
        for b in range(NB):
            scaled[1 + s, :, b * BLK : (b + 1) * BLK] = (feats[1 + s] * wcol[b]).astype(BF16)

    slots = pt_ref.shape[1]
    used = lax.broadcasted_iota(jnp.int32, (1, slots), 1) < pc_ref[...]
    hit_source = ps_ref[...] == lax.broadcasted_iota(jnp.int32, (8, slots), 0)
    lane = lax.broadcasted_iota(jnp.int32, (8, BLK), 1)
    for t in range(2):
        cols = []
        for h in range(2):
            hit = hit_source & (used & (pt_ref[...] == 2 * t + h))
            cols.append(jnp.sum(jnp.where(hit, 1.0, 0.0), axis=1, keepdims=True))
        live[t] = jnp.where(lane < CELL, cols[0], cols[1])

    msg[...] = jnp.zeros_like(msg)

    root3 = math.sqrt(3.0)
    root15 = math.sqrt(15.0)
    root5 = math.sqrt(5.0)
    sub16 = lax.broadcasted_iota(jnp.int32, (16, BLK), 0)
    lane16 = lax.broadcasted_iota(jnp.int32, (16, BLK), 1)

    def produce(p, t, s):
        lanes = pl.ds(pl.multiple_of(t * BLK, BLK), BLK)
        targets = [jnp.broadcast_to(pos_ref[d, :, lanes], (16, BLK)) for d in range(3)]
        shift = jnp.where(s == t + 1, 0, 2 * BLK)

        def chunk(q, c):
            r0 = pl.multiple_of(q * 16, 16)
            rows = pl.ds(r0, 16)
            ux, uy, uz = [(targets[d] - scol[s, d, rows, :]) * 0.2 for d in range(3)]
            square = ux * ux + uy * uy + uz * uz
            alive = jnp.broadcast_to(live[t, pl.ds(2 * s + q // 4, 1), :], (16, BLK)) > 0.5
            keep = (square < 1.0) & alive & (sub16 + (r0 + shift) != lane16)
            square = jnp.where(keep, square, 1.0)
            ux = jnp.where(keep, ux, 0.0)
            uy = jnp.where(keep, uy, 0.0)
            uz = jnp.where(keep, uz, 0.0)
            cosine2 = 2.0 * horner(COS_TERMS, square)
            gap = 1.0 - square
            base = (gap * gap) * (0.25 * horner(SINC_TERMS, square))
            ux15 = root15 * ux
            harmonic = [
                None,
                root3 * ux,
                root3 * uy,
                root3 * uz,
                ux15 * uy,
                root15 * uy * uz,
                (0.5 * root5) * (3.0 * uz * uz - square),
                ux15 * uz,
                (0.5 * root15) * (ux * ux - uy * uy),
            ]
            older, newer = None, base
            for b in range(NB):
                radial = newer * (1.0 / (b + 1)) if b else newer
                at = pl.ds(b * BLK + r0, 16)
                for y in range(NY):
                    value = radial * harmonic[y] if y else radial
                    table[p, at, y * BLK : (y + 1) * BLK] = value.astype(BF16)
                following = cosine2 * newer - older if b else cosine2 * newer
                older, newer = newer, following
            return c

        lax.fori_loop(0, BLK // 16, chunk, 0, unroll=True)

    def forward(p, t, s):
        produce(p, t, s)
        msg[t] += nn_dot(scaled[s], table[p])

    forward(1, 0, 1)

    total = plane - 1 + (zlo - 1) + (zhi - 1)
    total = total + has_left.astype(jnp.int32) + has_right.astype(jnp.int32)
    total = total + 2 * (me > 0).astype(jnp.int32)
    pl.semaphore_wait(barrier, total)

    to_left = remote(halo_out.at[0], halo_in.at[1], 0, (sp - 1, dp))
    to_right = remote(halo_out.at[1], halo_in.at[0], 1, (sp + 1, dp))

    @pl.when(has_left)
    def _():
        to_left.start()

    @pl.when(has_right)
    def _():
        to_right.start()

    def inner(p, c):
        forward(p, (p - 1) // 2, 1 + (p - 1) % 2)
        return c

    lax.fori_loop(2, 5, inner, 0)

    @pl.when(has_left)
    def _():
        to_right.wait_recv()

    @pl.when(has_right)
    def _():
        to_left.wait_recv()

    @pl.when(jnp.logical_not(has_left))
    def _():
        halo_in[0] = jnp.zeros((CH + 8, BLK), F32)

    @pl.when(jnp.logical_not(has_right))
    def _():
        halo_in[1] = jnp.zeros((CH + 8, BLK), F32)

    for h, s in ((0, 0), (1, 3)):
        feats[s] = halo_in[h, 0:CH, :]
        for d in range(3):
            scol[s, d] = column(halo_in[h, CH + d : CH + d + 1, :])
        for b in range(NB):
            scaled[s, :, b * BLK : (b + 1) * BLK] = (feats[s] * wcol[b]).astype(BF16)

    def outer(h, c):
        forward(5 * h, h, 3 * h)
        return c

    lax.fori_loop(0, 2, outer, 0)

    for fetch in fetches[6:]:
        fetch.wait()
    mix = mix_ref[...]
    mix_t = jnp.concatenate(
        [jnp.transpose(mix[k * CH : (k + 1) * CH].astype(F32)) for k in range(3)], axis=1
    ).astype(BF16)
    ro_col = column(ro_ref[...])
    for t in range(2):
        lanes = slice(t * BLK, (t + 1) * BLK)
        inv[0:CH, lanes] = msg[t, :, 0:BLK].astype(BF16)
        for k, ys in ((1, range(1, 4)), (2, range(4, 9))):
            acc = None
            for y in ys:
                m = msg[t, :, y * BLK : (y + 1) * BLK]
                acc = m * m if acc is None else acc + m * m
            inv[k * CH : (k + 1) * CH, lanes] = (0.5 * acc).astype(BF16)
    row_sp = lax.broadcasted_iota(jnp.int32, (NSPEC, BLK), 0)
    rog = jnp.zeros((CH, BLK), F32)
    shg = jnp.zeros((NSPEC, BLK), F32)
    for t in range(2):
        lanes = slice(t * BLK, (t + 1) * BLK)
        preact = nn_dot(mix_t, inv[:, lanes])
        gate = 1.0 / (1.0 + jnp.exp(-preact))
        updated = feats[1 + t] + preact * gate
        eg = eg_ref[:, lanes]
        rog += updated * eg
        shg += (spec_ref[:, lanes] == row_sp).astype(F32) * eg
        base = eg * ro_col
        upd[t] = updated
        gext[1 + t] = base
        gpre[:, lanes] = (base * gate * (1.0 + preact * (1.0 - gate))).astype(BF16)

    per = 3 * CH // plane
    mixg = nt_dot(inv[...], gpre[...])
    rog = jnp.sum(jnp.transpose(rog), axis=0, keepdims=True)
    shg = jnp.concatenate([shg, jnp.zeros((CH - NSPEC, BLK), F32)], axis=0)
    shg = jnp.sum(jnp.transpose(shg), axis=0, keepdims=True)
    for g in range(plane):
        big_src[g, 0:per, :] = mixg[g * per : (g + 1) * per]
        big_src[g, per : per + 1, :] = (rog, shg, jnp.zeros((1, BLK), F32))[min(g, 2)]

    def send_plane(src, dst, n):
        def step(k, c):
            g = plane_peer(k)
            remote(src(g), dst, n, at_plane(g)).start()
            return c

        lax.fori_loop(1, plane, step, 0)

    def wait_slots(buf, n, count, dev):
        part = buf.at[pl.ds(0, count)]
        return remote(part, part, n, dev)

    big_rs[me] = big_src[me]
    send_plane(lambda g: big_src.at[g], big_rs.at[me], 2)

    shift_col = jnp.transpose(jnp.broadcast_to(sh_ref[...], (NSPEC, NSPEC)))[:, 0:1]
    for t in range(2):
        lanes = slice(t * BLK, (t + 1) * BLK)
        onehot = (spec_ref[:, lanes] == row_sp).astype(F32)
        energy_ref[:, lanes] = jnp.sum(upd[t] * ro_col, axis=0, keepdims=True) + jnp.sum(
            onehot * shift_col, axis=0, keepdims=True
        )
        ginv = nn_dot(mix, gpre[:, lanes])
        gmsg[t, :, 0:BLK] = ginv[0:CH].astype(BF16)
        for y in range(1, NY):
            k = 1 if y < 4 else 2
            gmsg[t, :, y * BLK : (y + 1) * BLK] = (
                ginv[k * CH : (k + 1) * CH] * msg[t, :, y * BLK : (y + 1) * BLK]
            ).astype(BF16)

    stores[0].start()

    racc[...] = jnp.zeros_like(racc)

    def backward(s, parts):
        def step(n, c):
            rows = pl.ds(pl.multiple_of(n * 256, 256), 256)
            g = nt_dot(gmsg[parts[0][1]], table[parts[0][0], rows, :])
            for p, t in parts[1:]:
                g += nt_dot(gmsg[t], table[p, rows, :])
            here = feats[s]
            add = gext[s]
            for h in range(2):
                gb = g[:, h * BLK : (h + 1) * BLK]
                add += gb * wcol[2 * n + h]
                racc[2 * n + h] += gb * here
            gext[s] = add
            return c

        lax.fori_loop(0, NB // 2, step, 0, unroll=True)

    gext[0] = jnp.zeros((CH, BLK), F32)
    gext[3] = jnp.zeros((CH, BLK), F32)
    backward(0, [(0, 0)])
    backward(3, [(5, 1)])

    back_left = remote(gext.at[0], grad_in.at[1], 3, (sp - 1, dp))
    back_right = remote(gext.at[3], grad_in.at[0], 4, (sp + 1, dp))

    @pl.when(has_left)
    def _():
        back_left.start()

    @pl.when(has_right)
    def _():
        back_right.start()

    any_plane = at_plane(plane_peer(1))
    any_a = at_z(za_peer(1))
    any_b = at_z(zb_peer(1))

    backward(1, [(1, 0), (3, 1)])
    backward(2, [(2, 0), (4, 1)])

    sm_src[...] = jnp.concatenate(
        [jnp.sum(jnp.transpose(racc[b]), axis=0, keepdims=True) for b in range(NB)], axis=0
    )
    sm_pl[me] = sm_src[...]
    send_plane(lambda g: sm_src, sm_pl.at[me], 7)

    wait_slots(big_rs, 2, plane - 1, any_plane).wait_recv()
    z_as[...] = jnp.sum(big_rs[...], axis=0)
    z_a[zz % zlo] = z_as[...]
    for k in range(1, zlo):
        remote(z_as, z_a.at[zz % zlo], 5, at_z(za_peer(k))).start()

    wait_slots(z_a, 5, zlo - 1, any_a).wait_recv()
    z_bs[...] = jnp.sum(z_a[...], axis=0)
    z_b[zz // zlo] = z_bs[...]
    for k in range(1, zhi):
        remote(z_bs, z_b.at[zz // zlo], 6, at_z(zb_peer(k))).start()

    wait_slots(sm_pl, 7, plane - 1, any_plane).wait_recv()
    sm_sum[...] = jnp.sum(sm_pl[...], axis=0)
    slot = (zz + me) % nz
    to_z = remote(sm_sum, sm_x, 9, at_z((zz + nz - me) % nz))

    @pl.when(me > 0)
    def _():
        to_z.start()

    @pl.when(has_left)
    def _():
        back_right.wait_recv()
        gext[1] += grad_in[0]

    @pl.when(has_right)
    def _():
        back_left.wait_recv()
        gext[2] += grad_in[1]

    for t in range(2):
        fgrad_ref[0, :, t * BLK : (t + 1) * BLK] = gext[1 + t]
    stores[1].start()

    @pl.when(me > 0)
    def _():
        to_z.wait_recv()

    @pl.when(me == 0)
    def _():
        sm_x[...] = sm_sum[...]

    sm_z[slot] = sm_x[...]
    send_plane(lambda g: sm_x, sm_z.at[slot], 10)

    wait_slots(z_b, 6, zhi - 1, any_b).wait_recv()
    big_ag[me] = jnp.sum(z_b[...], axis=0)
    send_plane(lambda g: big_ag.at[me], big_ag.at[me], 8)

    scale = 1.0 / math.sqrt(2 * BLK * nsp * ndp)
    wait_slots(big_ag, 8, plane - 1, any_plane).wait_recv()
    for g in range(plane):
        mixg_ref[g * per : (g + 1) * per, :] = big_ag[g, 0:per, :] * scale
    rog_ref[...] = big_ag[0, per : per + 1, :] * scale
    shg_ref[...] = big_ag[1, per : per + 1, 0:NSPEC] * scale
    for store in stores[3:]:
        store.start()

    wait_slots(sm_z, 10, plane - 1, any_plane).wait_recv()
    rad_ref[...] = jnp.sum(sm_z[...], axis=0) * scale
    stores[2].start()
    for store in stores:
        store.wait()

    @pl.when(has_left)
    def _():
        to_left.wait_send()
        back_left.wait_send()

    @pl.when(has_right)
    def _():
        to_right.wait_send()
        back_right.wait_send()

    @pl.when(me > 0)
    def _():
        to_z.wait_send()

    wait_slots(big_rs, 2, plane - 1, any_plane).wait_send()
    wait_slots(z_a, 5, zlo - 1, any_a).wait_send()
    wait_slots(z_b, 6, zhi - 1, any_b).wait_send()
    wait_slots(sm_pl, 7, plane - 1, any_plane).wait_send()
    wait_slots(big_ag, 8, plane - 1, any_plane).wait_send()
    wait_slots(sm_z, 10, plane - 1, any_plane).wait_send()


def body(
    dims,
    node_features,
    positions,
    species,
    energy_cotangent,
    pair_target,
    pair_source,
    pair_count,
    radial_weight,
    mix_weight,
    readout_weight,
    species_shift,
):
    nsp, ndp, nxh, nz, zlo, ny, nco = dims
    plane = nxh * ndp * ny * nco
    zhi = nz // zlo
    per = 3 * CH // plane + 1
    atoms = 2 * BLK
    hbm = pl.BlockSpec(memory_space=pltpu.HBM)
    shapes = (
        jax.ShapeDtypeStruct((1, atoms), F32),
        jax.ShapeDtypeStruct((1, CH, atoms), F32),
        jax.ShapeDtypeStruct((NB, CH), F32),
        jax.ShapeDtypeStruct((3 * CH, CH), F32),
        jax.ShapeDtypeStruct((1, CH), F32),
        jax.ShapeDtypeStruct((1, NSPEC), F32),
    )
    outs = pl.pallas_call(
        functools.partial(kernel, dims),
        out_shape=shapes,
        in_specs=[hbm] * 11,
        out_specs=(hbm,) * 6,
        scratch_shapes=[
            pltpu.VMEM((6, NB * BLK, NY * BLK), BF16),
            pltpu.VMEM((4, CH, NB * BLK), BF16),
            pltpu.VMEM((4, CH, BLK), F32),
            pltpu.VMEM((4, 3, BLK, BLK), F32),
            pltpu.VMEM((NB, CH, BLK), F32),
            pltpu.VMEM((2, 8, BLK), F32),
            pltpu.VMEM((2, CH, NY * BLK), F32),
            pltpu.VMEM((2, CH, NY * BLK), BF16),
            pltpu.VMEM((3 * CH, atoms), BF16),
            pltpu.VMEM((2, CH, BLK), F32),
            pltpu.VMEM((CH, atoms), BF16),
            pltpu.VMEM((NB, CH, BLK), F32),
            pltpu.VMEM((4, CH, BLK), F32),
            pltpu.VMEM((2, CH + 8, BLK), F32),
            pltpu.VMEM((2, CH + 8, BLK), F32),
            pltpu.VMEM((2, CH, BLK), F32),
            pltpu.VMEM((plane, per, CH), F32),
            pltpu.VMEM((plane, per, CH), F32),
            pltpu.VMEM((zlo, per, CH), F32),
            pltpu.VMEM((zhi, per, CH), F32),
            pltpu.VMEM((per, CH), F32),
            pltpu.VMEM((per, CH), F32),
            pltpu.VMEM((plane, per, CH), F32),
            pltpu.VMEM((NB, CH), F32),
            pltpu.VMEM((plane, NB, CH), F32),
            pltpu.VMEM((NB, CH), F32),
            pltpu.VMEM((NB, CH), F32),
            pltpu.VMEM((nz, NB, CH), F32),
            pltpu.VMEM((1, CH, atoms), F32),
            pltpu.VMEM((3, 1, atoms), F32),
            pltpu.VMEM((1, atoms), jnp.int32),
            pltpu.VMEM((1, atoms), F32),
            pltpu.VMEM(pair_target.shape, jnp.int32),
            pltpu.VMEM(pair_target.shape, jnp.int32),
            pltpu.VMEM((1, 1), jnp.int32),
            pltpu.VMEM((NB, CH), F32),
            pltpu.VMEM((3 * CH, CH), BF16),
            pltpu.VMEM((1, CH), F32),
            pltpu.VMEM((1, NSPEC), F32),
            *(pltpu.VMEM(s.shape, s.dtype) for s in shapes),
            pltpu.SemaphoreType.DMA((11,)),
            pltpu.SemaphoreType.DMA((6,)),
            pltpu.SemaphoreType.DMA((11,)),
            pltpu.SemaphoreType.DMA((11,)),
        ],
        compiler_params=pltpu.CompilerParams(
            collective_id=0, has_side_effects=True, vmem_limit_bytes=64 << 20
        ),
    )(
        node_features,
        jnp.transpose(positions, (1, 0, 2)),
        species,
        energy_cotangent,
        pair_target,
        pair_source,
        pair_count,
        radial_weight,
        mix_weight,
        readout_weight.reshape(1, CH),
        species_shift.reshape(1, NSPEC),
    )
    energy, feature_grad, grad_radial, grad_mix, grad_out, grad_shift = pl.pallas_call(
        store_all,
        out_shape=shapes,
        in_specs=[pl.BlockSpec(memory_space=pltpu.VMEM)] * 6,
        out_specs=(hbm,) * 6,
        scratch_shapes=[pltpu.SemaphoreType.DMA((6,))],
        compiler_params=pltpu.CompilerParams(vmem_limit_bytes=64 << 20),
    )(*outs)
    return energy, feature_grad, grad_radial, grad_mix, grad_out.reshape(CH), grad_shift.reshape(NSPEC)


def solution(mesh):
    sizes = dict(mesh.shape)
    dims = (
        sizes["space"],
        sizes["dp"],
        SPLIT["xh"],
        SPLIT["z"],
        SPLIT["zlo"],
        SPLIT["y"],
        SPLIT["core"],
    )
    return jax.shard_map(
        functools.partial(body, dims),
        mesh=mesh,
        in_specs=(
            P("dp", None, "space"),
            P("dp", None, "space"),
            P("dp", "space"),
            P("dp", "space"),
            P("dp", "space"),
            P("dp", "space"),
            P("dp", "space"),
            P(),
            P(),
            P(),
            P(),
        ),
        out_specs=(P("dp", "space"), P("dp", None, "space"), P(), P(), P(), P()),
        check_vma=False,
    )
```

```python
import functools
import math

import jax
import jax.numpy as jnp
from jax import lax
from jax.experimental import pallas as pl
from jax.experimental.pallas import tpu as pltpu
from jax.sharding import PartitionSpec as P

CH = 128
NB = 8
NY = 9
NSPEC = 8
CELL = 64
BLK = 128
F32 = jnp.float32
BF16 = jnp.bfloat16
MESH = pl.DeviceIdType.MESH

SPLIT = {"xh": 2, "z": 32, "zlo": 4, "y": 4, "core": 2}

COS_TERMS = [(-1.0) ** k * math.pi ** (2 * k) / math.factorial(2 * k) for k in range(11)]
SINC_TERMS = [(-1.0) ** k * math.pi ** (2 * k) / math.factorial(2 * k + 1) for k in range(10)]


def horner(terms, x):
    total = x * terms[-1] + terms[-2]
    for term in reversed(terms[:-2]):
        total = total * x + term
    return total


def nt_dot(a, b):
    return lax.dot_general(a, b, (((1,), (1,)), ((), ())), preferred_element_type=F32)


def nn_dot(a, b):
    return jnp.dot(a, b, preferred_element_type=F32)


def column(row):
    return jnp.transpose(jnp.broadcast_to(row, (BLK, BLK)))


def store_all(*refs):
    sources, targets, sem = refs[:6], refs[6:12], refs[12]
    copies = [pltpu.make_async_copy(s, t, sem.at[n]) for n, (s, t) in enumerate(zip(sources, targets))]
    for copy in copies:
        copy.start()
    for copy in copies:
        copy.wait()


def kernel(
    dims,
    feat_hbm,
    pos_hbm,
    spec_hbm,
    eg_hbm,
    pt_hbm,
    ps_hbm,
    pc_hbm,
    w_hbm,
    mix_hbm,
    ro_hbm,
    sh_hbm,
    energy_hbm,
    fgrad_hbm,
    rad_hbm,
    mixg_hbm,
    rog_hbm,
    shg_hbm,
    table,
    scaled,
    feats,
    scol,
    wcol,
    live,
    msg,
    gmsg,
    inv,
    mixt,
    roc,
    upd,
    gpre,
    racc,
    gext,
    halo_out,
    halo_in,
    grad_in,
    big_src,
    big_rs,
    z_a,
    z_b,
    z_as,
    z_bs,
    big_ag,
    sm_src,
    sm_pl,
    sm_sum,
    sm_x,
    sm_z,
    feat_ref,
    pos_ref,
    spec_ref,
    eg_ref,
    pt_ref,
    ps_ref,
    pc_ref,
    w_ref,
    mix_ref,
    ro_ref,
    sh_ref,
    energy_ref,
    fgrad_ref,
    rad_ref,
    mixg_ref,
    rog_ref,
    shg_ref,
    in_sem,
    out_sem,
    send_sem,
    recv_sem,
):
    nsp, ndp, nxh, nz, zlo, ny, nco = dims
    plane = nxh * ndp * ny * nco
    zhi = nz // zlo
    sp = lax.axis_index("space")
    dp = lax.axis_index("dp")
    core = sp % nco
    yy = (sp // nco) % ny
    zz = (sp // (nco * ny)) % nz
    xh = sp // (nco * ny * nz)
    me = ((xh * ndp + dp) * ny + yy) * nco + core

    def at_plane(g):
        return (
            ((g // (nco * ny * ndp)) * nz + zz) * (ny * nco) + g % (nco * ny),
            (g // (nco * ny)) % ndp,
        )

    def at_z(z):
        return ((xh * nz + z) * ny + yy) * nco + core, dp

    def plane_peer(k):
        return (me + k) % plane

    def za_peer(k):
        return (zz // zlo) * zlo + (zz % zlo + k) % zlo

    def zb_peer(k):
        return ((zz // zlo + k) % zhi) * zlo + zz % zlo

    def remote(src, dst, n, dev):
        return pltpu.make_async_remote_copy(
            src_ref=src,
            dst_ref=dst,
            send_sem=send_sem.at[n],
            recv_sem=recv_sem.at[n],
            device_id=dev,
            device_id_type=MESH,
        )

    fetches = [
        pltpu.make_async_copy(src, dst, in_sem.at[n])
        for n, (src, dst) in enumerate(
            (
                (feat_hbm, feat_ref),
                (pos_hbm, pos_ref),
                (pt_hbm, pt_ref),
                (ps_hbm, ps_ref),
                (pc_hbm, pc_ref),
                (w_hbm, w_ref),
                (eg_hbm, eg_ref),
                (spec_hbm, spec_ref),
                (mix_hbm, mix_ref),
                (ro_hbm, ro_ref),
                (sh_hbm, sh_ref),
            )
        )
    ]
    for fetch in fetches:
        fetch.start()
    stores = [
        pltpu.make_async_copy(src, dst, out_sem.at[n])
        for n, (src, dst) in enumerate(
            (
                (energy_ref, energy_hbm),
                (fgrad_ref, fgrad_hbm),
                (rad_ref, rad_hbm),
                (mixg_ref, mixg_hbm),
                (rog_ref, rog_hbm),
                (shg_ref, shg_hbm),
            )
        )
    ]

    barrier = pltpu.get_barrier_semaphore()

    def greet(dev):
        pl.semaphore_signal(barrier, inc=1, device_id=dev, device_id_type=MESH)

    has_left = sp > 0
    has_right = sp < nsp - 1

    @pl.when(has_left)
    def _():
        greet((sp - 1, dp))

    @pl.when(has_right)
    def _():
        greet((sp + 1, dp))

    def greet_plane(k, c):
        greet(at_plane(plane_peer(k)))
        return c

    lax.fori_loop(1, plane, greet_plane, 0)
    for k in range(1, zlo):
        greet(at_z(za_peer(k)))
    for k in range(1, zhi):
        greet(at_z(zb_peer(k)))

    @pl.when(me > 0)
    def _():
        greet(at_z((zz + me) % nz))
        greet(at_z((zz + nz - me) % nz))

    for fetch in fetches[:6]:
        fetch.wait()
    features = feat_ref[0]
    for s in range(2):
        halo_out[s, 0:CH, :] = features[:, s * BLK : (s + 1) * BLK]
        for d in range(3):
            halo_out[s, CH + d : CH + d + 1, :] = pos_ref[d, :, s * BLK : (s + 1) * BLK]
        halo_out[s, CH + 3 : CH + 8, :] = jnp.zeros((5, BLK), F32)
        feats[1 + s] = features[:, s * BLK : (s + 1) * BLK]
        for d in range(3):
            scol[1 + s, d] = column(pos_ref[d, :, s * BLK : (s + 1) * BLK])

    for b in range(NB):
        wcol[b] = column(w_ref[b : b + 1, :])
    for s in range(2):
        for b in range(NB):
            scaled[1 + s, :, b * BLK : (b + 1) * BLK] = (feats[1 + s] * wcol[b]).astype(BF16)

    slots = pt_ref.shape[1]
    used = lax.broadcasted_iota(jnp.int32, (1, slots), 1) < pc_ref[...]
    hit_source = ps_ref[...] == lax.broadcasted_iota(jnp.int32, (8, slots), 0)
    lane = lax.broadcasted_iota(jnp.int32, (8, BLK), 1)
    for t in range(2):
        cols = []
        for h in range(2):
            hit = hit_source & (used & (pt_ref[...] == 2 * t + h))
            cols.append(jnp.sum(jnp.where(hit, 1.0, 0.0), axis=1, keepdims=True))
        live[t] = jnp.where(lane < CELL, cols[0], cols[1])

    msg[...] = jnp.zeros_like(msg)

    root3 = math.sqrt(3.0)
    root15 = math.sqrt(15.0)
    root5 = math.sqrt(5.0)
    sub16 = lax.broadcasted_iota(jnp.int32, (16, BLK), 0)
    lane16 = lax.broadcasted_iota(jnp.int32, (16, BLK), 1)

    def produce(p, t, s):
        lanes = pl.ds(pl.multiple_of(t * BLK, BLK), BLK)
        targets = [jnp.broadcast_to(pos_ref[d, :, lanes], (16, BLK)) for d in range(3)]
        shift = jnp.where(s == t + 1, 0, 2 * BLK)

        def chunk(q, c):
            r0 = pl.multiple_of(q * 16, 16)
            rows = pl.ds(r0, 16)
            ux, uy, uz = [(targets[d] - scol[s, d, rows, :]) * 0.2 for d in range(3)]
            square = ux * ux + uy * uy + uz * uz
            alive = jnp.broadcast_to(live[t, pl.ds(2 * s + q // 4, 1), :], (16, BLK)) > 0.5
            keep = (square < 1.0) & alive & (sub16 + (r0 + shift) != lane16)
            square = jnp.where(keep, square, 1.0)
            ux = jnp.where(keep, ux, 0.0)
            uy = jnp.where(keep, uy, 0.0)
            uz = jnp.where(keep, uz, 0.0)
            cosine2 = 2.0 * horner(COS_TERMS, square)
            gap = 1.0 - square
            base = (gap * gap) * (0.25 * horner(SINC_TERMS, square))
            ux15 = root15 * ux
            harmonic = [
                None,
                root3 * ux,
                root3 * uy,
                root3 * uz,
                ux15 * uy,
                root15 * uy * uz,
                (0.5 * root5) * (3.0 * uz * uz - square),
                ux15 * uz,
                (0.5 * root15) * (ux * ux - uy * uy),
            ]
            older, newer = None, base
            for b in range(NB):
                radial = newer * (1.0 / (b + 1)) if b else newer
                at = pl.ds(b * BLK + r0, 16)
                for y in range(NY):
                    value = radial * harmonic[y] if y else radial
                    table[p, at, y * BLK : (y + 1) * BLK] = value.astype(BF16)
                following = cosine2 * newer - older if b else cosine2 * newer
                older, newer = newer, following
            return c

        lax.fori_loop(0, BLK // 16, chunk, 0, unroll=True)

    def forward(p, t, s):
        produce(p, t, s)
        msg[t] += nn_dot(scaled[s], table[p])

    forward(1, 0, 1)

    for fetch in fetches[6:]:
        fetch.wait()
    for k in range(3):
        rows = slice(k * CH, (k + 1) * CH)
        mixt[:, rows] = jnp.transpose(mix_ref[rows, :].astype(F32)).astype(BF16)
    roc[...] = column(ro_ref[...])

    total = plane - 1 + (zlo - 1) + (zhi - 1)
    total = total + has_left.astype(jnp.int32) + has_right.astype(jnp.int32)
    total = total + 2 * (me > 0).astype(jnp.int32)
    pl.semaphore_wait(barrier, total)

    to_left = remote(halo_out.at[0], halo_in.at[1], 0, (sp - 1, dp))
    to_right = remote(halo_out.at[1], halo_in.at[0], 1, (sp + 1, dp))

    @pl.when(has_left)
    def _():
        to_left.start()

    @pl.when(has_right)
    def _():
        to_right.start()

    def inner(p, c):
        forward(p, (p - 1) // 2, 1 + (p - 1) % 2)
        return c

    lax.fori_loop(2, 5, inner, 0)

    @pl.when(has_left)
    def _():
        to_right.wait_recv()

    @pl.when(has_right)
    def _():
        to_left.wait_recv()

    @pl.when(jnp.logical_not(has_left))
    def _():
        halo_in[0] = jnp.zeros((CH + 8, BLK), F32)

    @pl.when(jnp.logical_not(has_right))
    def _():
        halo_in[1] = jnp.zeros((CH + 8, BLK), F32)

    for h, s in ((0, 0), (1, 3)):
        feats[s] = halo_in[h, 0:CH, :]
        for d in range(3):
            scol[s, d] = column(halo_in[h, CH + d : CH + d + 1, :])
        for b in range(NB):
            scaled[s, :, b * BLK : (b + 1) * BLK] = (feats[s] * wcol[b]).astype(BF16)

    def outer(h, c):
        forward(5 * h, h, 3 * h)
        return c

    lax.fori_loop(0, 2, outer, 0)

    mix = mix_ref[...]
    mix_t = mixt[...]
    ro_col = roc[...]
    for t in range(2):
        lanes = slice(t * BLK, (t + 1) * BLK)
        inv[0:CH, lanes] = msg[t, :, 0:BLK].astype(BF16)
        for k, ys in ((1, range(1, 4)), (2, range(4, 9))):
            acc = None
            for y in ys:
                m = msg[t, :, y * BLK : (y + 1) * BLK]
                acc = m * m if acc is None else acc + m * m
            inv[k * CH : (k + 1) * CH, lanes] = (0.5 * acc).astype(BF16)
    row_sp = lax.broadcasted_iota(jnp.int32, (NSPEC, BLK), 0)
    rog = jnp.zeros((CH, BLK), F32)
    shg = jnp.zeros((NSPEC, BLK), F32)
    for t in range(2):
        lanes = slice(t * BLK, (t + 1) * BLK)
        preact = nn_dot(mix_t, inv[:, lanes])
        gate = 1.0 / (1.0 + jnp.exp(-preact))
        updated = feats[1 + t] + preact * gate
        eg = eg_ref[:, lanes]
        rog += updated * eg
        shg += (spec_ref[:, lanes] == row_sp).astype(F32) * eg
        base = eg * ro_col
        upd[t] = updated
        gext[1 + t] = base
        gpre[:, lanes] = (base * gate * (1.0 + preact * (1.0 - gate))).astype(BF16)

    per = 3 * CH // plane
    mixg = nt_dot(inv[...], gpre[...])
    rog = jnp.sum(jnp.transpose(rog), axis=0, keepdims=True)
    shg = jnp.concatenate([shg, jnp.zeros((CH - NSPEC, BLK), F32)], axis=0)
    shg = jnp.sum(jnp.transpose(shg), axis=0, keepdims=True)
    for g in range(plane):
        big_src[g, 0:per, :] = mixg[g * per : (g + 1) * per]
        big_src[g, per : per + 1, :] = (rog, shg, jnp.zeros((1, BLK), F32))[min(g, 2)]

    def send_plane(src, dst, n):
        def step(k, c):
            g = plane_peer(k)
            remote(src(g), dst, n, at_plane(g)).start()
            return c

        lax.fori_loop(1, plane, step, 0)

    def wait_slots(buf, n, count, dev):
        part = buf.at[pl.ds(0, count)]
        return remote(part, part, n, dev)

    big_rs[me] = big_src[me]
    send_plane(lambda g: big_src.at[g], big_rs.at[me], 2)

    shift_col = jnp.transpose(jnp.broadcast_to(sh_ref[...], (NSPEC, NSPEC)))[:, 0:1]
    for t in range(2):
        lanes = slice(t * BLK, (t + 1) * BLK)
        onehot = (spec_ref[:, lanes] == row_sp).astype(F32)
        energy_ref[:, lanes] = jnp.sum(upd[t] * ro_col, axis=0, keepdims=True) + jnp.sum(
            onehot * shift_col, axis=0, keepdims=True
        )
        ginv = nn_dot(mix, gpre[:, lanes])
        gmsg[t, :, 0:BLK] = ginv[0:CH].astype(BF16)
        for y in range(1, NY):
            k = 1 if y < 4 else 2
            gmsg[t, :, y * BLK : (y + 1) * BLK] = (
                ginv[k * CH : (k + 1) * CH] * msg[t, :, y * BLK : (y + 1) * BLK]
            ).astype(BF16)

    stores[0].start()

    racc[...] = jnp.zeros_like(racc)

    def backward(s, parts):
        def step(n, c):
            rows = pl.ds(pl.multiple_of(n * 256, 256), 256)
            g = nt_dot(gmsg[parts[0][1]], table[parts[0][0], rows, :])
            for p, t in parts[1:]:
                g += nt_dot(gmsg[t], table[p, rows, :])
            here = feats[s]
            add = gext[s]
            for h in range(2):
                gb = g[:, h * BLK : (h + 1) * BLK]
                add += gb * wcol[2 * n + h]
                racc[2 * n + h] += gb * here
            gext[s] = add
            return c

        lax.fori_loop(0, NB // 2, step, 0, unroll=True)

    gext[0] = jnp.zeros((CH, BLK), F32)
    gext[3] = jnp.zeros((CH, BLK), F32)
    backward(0, [(0, 0)])
    backward(3, [(5, 1)])

    back_left = remote(gext.at[0], grad_in.at[1], 3, (sp - 1, dp))
    back_right = remote(gext.at[3], grad_in.at[0], 4, (sp + 1, dp))

    @pl.when(has_left)
    def _():
        back_left.start()

    @pl.when(has_right)
    def _():
        back_right.start()

    any_plane = at_plane(plane_peer(1))
    any_a = at_z(za_peer(1))
    any_b = at_z(zb_peer(1))

    backward(1, [(1, 0), (3, 1)])
    backward(2, [(2, 0), (4, 1)])

    sm_src[...] = jnp.concatenate(
        [jnp.sum(jnp.transpose(racc[b]), axis=0, keepdims=True) for b in range(NB)], axis=0
    )
    sm_pl[me] = sm_src[...]
    send_plane(lambda g: sm_src, sm_pl.at[me], 7)

    wait_slots(big_rs, 2, plane - 1, any_plane).wait_recv()
    z_as[...] = jnp.sum(big_rs[...], axis=0)
    z_a[zz % zlo] = z_as[...]
    for k in range(1, zlo):
        remote(z_as, z_a.at[zz % zlo], 5, at_z(za_peer(k))).start()

    wait_slots(z_a, 5, zlo - 1, any_a).wait_recv()
    z_bs[...] = jnp.sum(z_a[...], axis=0)
    z_b[zz // zlo] = z_bs[...]
    for k in range(1, zhi):
        remote(z_bs, z_b.at[zz // zlo], 6, at_z(zb_peer(k))).start()

    wait_slots(sm_pl, 7, plane - 1, any_plane).wait_recv()
    sm_sum[...] = jnp.sum(sm_pl[...], axis=0)
    slot = (zz + me) % nz
    to_z = remote(sm_sum, sm_x, 9, at_z((zz + nz - me) % nz))

    @pl.when(me > 0)
    def _():
        to_z.start()

    @pl.when(has_left)
    def _():
        back_right.wait_recv()
        gext[1] += grad_in[0]

    @pl.when(has_right)
    def _():
        back_left.wait_recv()
        gext[2] += grad_in[1]

    for t in range(2):
        fgrad_ref[0, :, t * BLK : (t + 1) * BLK] = gext[1 + t]
    stores[1].start()

    @pl.when(me > 0)
    def _():
        to_z.wait_recv()

    @pl.when(me == 0)
    def _():
        sm_x[...] = sm_sum[...]

    sm_z[slot] = sm_x[...]
    send_plane(lambda g: sm_x, sm_z.at[slot], 10)

    wait_slots(z_b, 6, zhi - 1, any_b).wait_recv()
    big_ag[me] = jnp.sum(z_b[...], axis=0)
    send_plane(lambda g: big_ag.at[me], big_ag.at[me], 8)

    scale = 1.0 / math.sqrt(2 * BLK * nsp * ndp)
    wait_slots(big_ag, 8, plane - 1, any_plane).wait_recv()
    for g in range(plane):
        mixg_ref[g * per : (g + 1) * per, :] = big_ag[g, 0:per, :] * scale
    rog_ref[...] = big_ag[0, per : per + 1, :] * scale
    shg_ref[...] = big_ag[1, per : per + 1, 0:NSPEC] * scale
    for store in stores[3:]:
        store.start()

    wait_slots(sm_z, 10, plane - 1, any_plane).wait_recv()
    rad_ref[...] = jnp.sum(sm_z[...], axis=0) * scale
    stores[2].start()
    for store in stores:
        store.wait()

    @pl.when(has_left)
    def _():
        to_left.wait_send()
        back_left.wait_send()

    @pl.when(has_right)
    def _():
        to_right.wait_send()
        back_right.wait_send()

    @pl.when(me > 0)
    def _():
        to_z.wait_send()

    wait_slots(big_rs, 2, plane - 1, any_plane).wait_send()
    wait_slots(z_a, 5, zlo - 1, any_a).wait_send()
    wait_slots(z_b, 6, zhi - 1, any_b).wait_send()
    wait_slots(sm_pl, 7, plane - 1, any_plane).wait_send()
    wait_slots(big_ag, 8, plane - 1, any_plane).wait_send()
    wait_slots(sm_z, 10, plane - 1, any_plane).wait_send()


def body(
    dims,
    node_features,
    positions,
    species,
    energy_cotangent,
    pair_target,
    pair_source,
    pair_count,
    radial_weight,
    mix_weight,
    readout_weight,
    species_shift,
):
    nsp, ndp, nxh, nz, zlo, ny, nco = dims
    plane = nxh * ndp * ny * nco
    zhi = nz // zlo
    per = 3 * CH // plane + 1
    atoms = 2 * BLK
    hbm = pl.BlockSpec(memory_space=pltpu.HBM)
    shapes = (
        jax.ShapeDtypeStruct((1, atoms), F32),
        jax.ShapeDtypeStruct((1, CH, atoms), F32),
        jax.ShapeDtypeStruct((NB, CH), F32),
        jax.ShapeDtypeStruct((3 * CH, CH), F32),
        jax.ShapeDtypeStruct((1, CH), F32),
        jax.ShapeDtypeStruct((1, NSPEC), F32),
    )
    outs = pl.pallas_call(
        functools.partial(kernel, dims),
        out_shape=shapes,
        in_specs=[hbm] * 11,
        out_specs=(hbm,) * 6,
        scratch_shapes=[
            pltpu.VMEM((6, NB * BLK, NY * BLK), BF16),
            pltpu.VMEM((4, CH, NB * BLK), BF16),
            pltpu.VMEM((4, CH, BLK), F32),
            pltpu.VMEM((4, 3, BLK, BLK), F32),
            pltpu.VMEM((NB, CH, BLK), F32),
            pltpu.VMEM((2, 8, BLK), F32),
            pltpu.VMEM((2, CH, NY * BLK), F32),
            pltpu.VMEM((2, CH, NY * BLK), BF16),
            pltpu.VMEM((3 * CH, atoms), BF16),
            pltpu.VMEM((CH, 3 * CH), BF16),
            pltpu.VMEM((CH, BLK), F32),
            pltpu.VMEM((2, CH, BLK), F32),
            pltpu.VMEM((CH, atoms), BF16),
            pltpu.VMEM((NB, CH, BLK), F32),
            pltpu.VMEM((4, CH, BLK), F32),
            pltpu.VMEM((2, CH + 8, BLK), F32),
            pltpu.VMEM((2, CH + 8, BLK), F32),
            pltpu.VMEM((2, CH, BLK), F32),
            pltpu.VMEM((plane, per, CH), F32),
            pltpu.VMEM((plane, per, CH), F32),
            pltpu.VMEM((zlo, per, CH), F32),
            pltpu.VMEM((zhi, per, CH), F32),
            pltpu.VMEM((per, CH), F32),
            pltpu.VMEM((per, CH), F32),
            pltpu.VMEM((plane, per, CH), F32),
            pltpu.VMEM((NB, CH), F32),
            pltpu.VMEM((plane, NB, CH), F32),
            pltpu.VMEM((NB, CH), F32),
            pltpu.VMEM((NB, CH), F32),
            pltpu.VMEM((nz, NB, CH), F32),
            pltpu.VMEM((1, CH, atoms), F32),
            pltpu.VMEM((3, 1, atoms), F32),
            pltpu.VMEM((1, atoms), jnp.int32),
            pltpu.VMEM((1, atoms), F32),
            pltpu.VMEM(pair_target.shape, jnp.int32),
            pltpu.VMEM(pair_target.shape, jnp.int32),
            pltpu.VMEM((1, 1), jnp.int32),
            pltpu.VMEM((NB, CH), F32),
            pltpu.VMEM((3 * CH, CH), BF16),
            pltpu.VMEM((1, CH), F32),
            pltpu.VMEM((1, NSPEC), F32),
            *(pltpu.VMEM(s.shape, s.dtype) for s in shapes),
            pltpu.SemaphoreType.DMA((11,)),
            pltpu.SemaphoreType.DMA((6,)),
            pltpu.SemaphoreType.DMA((11,)),
            pltpu.SemaphoreType.DMA((11,)),
        ],
        compiler_params=pltpu.CompilerParams(
            collective_id=0, has_side_effects=True, vmem_limit_bytes=64 << 20
        ),
    )(
        node_features,
        jnp.transpose(positions, (1, 0, 2)),
        species,
        energy_cotangent,
        pair_target,
        pair_source,
        pair_count,
        radial_weight,
        mix_weight,
        readout_weight.reshape(1, CH),
        species_shift.reshape(1, NSPEC),
    )
    energy, feature_grad, grad_radial, grad_mix, grad_out, grad_shift = pl.pallas_call(
        store_all,
        out_shape=shapes,
        in_specs=[pl.BlockSpec(memory_space=pltpu.VMEM)] * 6,
        out_specs=(hbm,) * 6,
        scratch_shapes=[pltpu.SemaphoreType.DMA((6,))],
        compiler_params=pltpu.CompilerParams(vmem_limit_bytes=64 << 20),
    )(*outs)
    return energy, feature_grad, grad_radial, grad_mix, grad_out.reshape(CH), grad_shift.reshape(NSPEC)


def solution(mesh):
    sizes = dict(mesh.shape)
    dims = (
        sizes["space"],
        sizes["dp"],
        SPLIT["xh"],
        SPLIT["z"],
        SPLIT["zlo"],
        SPLIT["y"],
        SPLIT["core"],
    )
    return jax.shard_map(
        functools.partial(body, dims),
        mesh=mesh,
        in_specs=(
            P("dp", None, "space"),
            P("dp", None, "space"),
            P("dp", "space"),
            P("dp", "space"),
            P("dp", "space"),
            P("dp", "space"),
            P("dp", "space"),
            P(),
            P(),
            P(),
            P(),
        ),
        out_specs=(P("dp", "space"), P("dp", None, "space"), P(), P(), P(), P()),
        check_vma=False,
    )
```
